32 devices in a mesh: sky: 2 (over y), ma: 4 (over z), freq: 2 (over x), pol: 2 (over core).
Axes of the slice: x: 2, y: 2, z: 4, core: 2. Of those that a mesh axis runs over, the one named last changes fastest.
Arguments:
- alm: bfloat16 [2, 2, 1024, 4, 1024], P(None, 'freq', ('ma', 'pol'), None, 'sky'), parts along dimension 4, may hold values from -6 to 6
- beam: bfloat16 [4, 2, 2, 1024, 1024], P('ma', 'freq', None, 'pol'), may hold values from -0.1875 to 0.1875
- m_table: int32 [4], P('ma'), may hold values from 0 to 511, as said below
- chan_mask: int32 [2], P('freq'), may hold values from 0 to 1, as said below
- noise: float32 [2, 1024], P('freq', 'pol'), may hold values from 0.5 to 4
Outputs:
- scaled: bfloat16 [2, 2, 4, 1024, 1024], P(None, 'freq', 'ma', 'pol', 'sky'), parts along dimension 4
- channel_power: float32 [4], P(('sky', 'freq')), parts along dimension 0
The draws below stay inside these ranges and needn't reach their ends.
There are 2 independent parts, one for each index of `sky`. The reference program is written for one: setup_inputs(seed, part) draws one part's arguments, and reference() takes and returns one part's arrays. A program takes and returns all parts, laid end to end along the dimension named above; an argument that names none is the same for every part. Nothing has to cross between parts.
Inputs may be any that keep to these rules, and one draw needn't show every extreme that they name: `m_table`: the 4 values are distinct whole numbers below 512. `chan_mask`: at least one of the 2 channels is usable.
All inputs are finite; a program needn't handle non-finite values.
Results may differ from the reference program's by a relative error of at most 0.00055.
Values may be sent and summed in bfloat16 or wider, within the bound.
No kernel may reach another device: no remote copies, remote signals or barrier semaphores. Data moves between devices by JAX's collectives and lax.ppermute only.
A program may use at most 64 MiB of HBM per device.

```python
import math
import jax
import jax.numpy as jnp
from jax import lax

L = 1024
K = 1024
S = 512
M = 4
F = 2


def draw_m_table(key, part):
    return jax.random.permutation(key, L // 2)[:M].astype(jnp.int32)


def draw_chan_mask(key, part):
    mask_key = jax.random.fold_in(key, 23)
    first_key, second_key = jax.random.split(mask_key)
    flags = (jax.random.randint(first_key, (F,), 0, 4) < 3).astype(jnp.int32)
    chosen = jax.random.randint(second_key, (), 0, F)
    forced = (jnp.arange(F, dtype=jnp.int32) == chosen).astype(jnp.int32)
    return jnp.maximum(flags, forced).astype(jnp.int32)


def block_scale(stream_key, shape, pieces, least, top_value):
    loudness, own = 1.0, jax.random.fold_in(stream_key, 6)
    for dim, parts in pieces:
        draws = jnp.exp(jax.random.uniform(jax.random.fold_in(own, dim), (parts,), jnp.float32, least / len(pieces), top_value / len(pieces)))
        loudness = loudness * jnp.repeat(draws, shape[dim] // parts).reshape([-1 if axis == dim else 1 for axis in range(len(shape))])
    return loudness


def scatter_about(rng, dims, spread, reach, shards=(), held_as=jnp.bfloat16):
    result = spread * jax.random.normal(rng, dims, jnp.float32)
    if shards:
        result = result * block_scale(rng, dims, shards, -0.22, 0.18)
    return jnp.clip(result, -reach, reach).astype(held_as)


def setup_inputs(seed: int = 0, part: int = 0) -> dict:
    key_of = jax.random.split(jax.random.key(seed), 6)
    part_keys = jax.random.split(jax.random.fold_in(key_of[5], part), 6)
    return {
        "alm": scatter_about(part_keys[0], (2, F, L, M, S), 1.0, 6.0, ((1, 2), (2, 8))),
        "beam": scatter_about(key_of[1], (M, F, 2, K, L), L ** -0.5, 0.1875, ((0, 4), (1, 2), (3, 2))),
        "m_table": draw_m_table(jax.random.fold_in(key_of[5], 71), part),
        "chan_mask": draw_chan_mask(jax.random.fold_in(key_of[5], 71), part),
        "noise": jnp.clip(jnp.exp(math.log(4.0) - 2.0794415 * jax.random.uniform(key_of[4], (F, K), jnp.float32) ** block_scale(key_of[4], (F, K), ((0, 2), (1, 2)), -0.2, 0.2)), 0.5, 4.0),
    }


def reference(alm, beam, m_table, chan_mask, noise):
    degree = jnp.arange(L, dtype=jnp.int32)

    def one_mode(inputs):
        response, coeffs, m_value = inputs
        keep_mask = (degree >= m_value)[None, None, :, None]
        active = jnp.where(keep_mask, coeffs, jnp.zeros((), coeffs.dtype)).astype(jnp.float32)
        response = response.astype(jnp.float32)
        real_part = jnp.einsum('fkl,fls->fks', response[:, 0], active[0]) - jnp.einsum('fkl,fls->fks', response[:, 1], active[1])
        imag_part = jnp.einsum('fkl,fls->fks', response[:, 0], active[1]) + jnp.einsum('fkl,fls->fks', response[:, 1], active[0])
        return jnp.stack([real_part, imag_part])
    per_mode = lax.map(one_mode, (beam, jnp.moveaxis(alm, 3, 0), m_table))
    visibility = jnp.transpose(per_mode, (1, 2, 0, 3, 4))
    weighted = visibility * visibility / noise[None, :, None, :, None]
    channel_power = lax.optimization_barrier(jnp.sum(weighted, axis=(0, 2, 3, 4))) / jnp.float32(M * K * S)
    mask_float = chan_mask.astype(jnp.float32)
    live_count = jnp.sum(mask_float)
    band_power = jnp.sum(mask_float * channel_power) / live_count
    factor = mask_float / jnp.sqrt(0.5 * channel_power + 0.5 * band_power + 1e-06)
    scaled = visibility * (lax.rsqrt(noise) * factor[:, None])[None, :, None, :, None]
    return (scaled.astype(jnp.bfloat16), channel_power)
```

```python
import functools

import jax
import jax.numpy as jnp
from jax import lax
from jax.experimental import pallas as pl
from jax.experimental.pallas import tpu as pltpu
from jax.sharding import PartitionSpec as P

VMEM = pl.BlockSpec(memory_space=pltpu.VMEM)
SMEM = pl.BlockSpec(memory_space=pltpu.SMEM)


def column(row):
    return jnp.transpose(jnp.broadcast_to(row, (128, row.shape[1])))


def contract(place_ref, beam_ref, block_refs, steps):
    ell = block_refs[0].shape[1]
    left, right_real, right_imag = [], [], []
    for ref, (step, other) in zip(block_refs, steps, strict=True):
        owner = place_ref[0] ^ step
        half = place_ref[1] ^ other
        start = (owner * place_ref[3] + half) * ell
        columns = pl.ds(pl.multiple_of(start, ell), ell)
        degree = start + lax.broadcasted_iota(jnp.int32, (ell, ref.shape[2]), 0)
        keep = degree >= place_ref[2]
        real = jnp.where(keep, ref[0], jnp.zeros((), ref.dtype))
        imag = jnp.where(keep, ref[1], jnp.zeros((), ref.dtype))
        left += [beam_ref[0, :, columns], beam_ref[1, :, columns]]
        right_real += [real, -imag]
        right_imag += [imag, real]
    left = jnp.concatenate(left, axis=1)
    dot = functools.partial(jnp.dot, preferred_element_type=jnp.float32)
    return (
        dot(left, jnp.concatenate(right_real, axis=0)),
        dot(left, jnp.concatenate(right_imag, axis=0)),
    )


def early_kernel(steps, place_ref, beam_ref, *refs):
    *blocks, vis_ref = refs
    vis_ref[0], vis_ref[1] = contract(place_ref, beam_ref, blocks, steps)


def late_kernel(steps, slots, place_ref, mask_ref, beam_ref, noise_ref, early_ref, *refs):
    *blocks, vis_ref, power_ref = refs
    real, imag = contract(place_ref, beam_ref, blocks, steps)
    real += early_ref[0]
    imag += early_ref[1]
    vis_ref[0] = real
    vis_ref[1] = imag
    squares = real * real + imag * imag
    folded = functools.reduce(
        jnp.add, [squares[:, i : i + 128] for i in range(0, squares.shape[1], 128)]
    )
    total = jnp.sum(folded / column(noise_ref[...]))
    lane = lax.broadcasted_iota(jnp.int32, power_ref.shape, 1)
    live = jnp.where(place_ref[4] == 0, mask_ref[0], 0).astype(jnp.float32)
    channel = place_ref[5]
    power_ref[...] = jnp.where(lane == channel, total, 0.0) + jnp.where(
        lane == channel + slots, live, 0.0
    )


def finish_kernel(slots, modes, place_ref, mask_ref, noise_ref, total_ref, vis_ref, scaled_ref, power_ref):
    lane = lax.broadcasted_iota(jnp.int32, (1, 128), 1)
    totals = total_ref[0:1, :]
    powers = totals / modes
    live = jnp.sum(jnp.where((lane >= slots) & (lane < 2 * slots), totals, 0.0))
    masks = pltpu.roll(totals, 128 - slots, 1)
    band = jnp.sum(jnp.where(lane < slots, powers * masks, 0.0))
    own = jnp.sum(jnp.where(lane == place_ref[5], powers, 0.0))
    mask = mask_ref[0].astype(jnp.float32)
    inner = jnp.full((1, noise_ref.shape[1]), 0.5 * own + 1e-06, jnp.float32)
    inner += 0.5 * (jnp.full_like(inner, band) / jnp.full_like(inner, live))
    factor = mask / jnp.sqrt(inner)
    scale = column(lax.rsqrt(noise_ref[...]) * factor)
    for c in range(vis_ref.shape[0]):
        for i in range(0, vis_ref.shape[2], 128):
            scaled_ref[c, :, i : i + 128] = (vis_ref[c, :, i : i + 128] * scale).astype(
                scaled_ref.dtype
            )
    power_ref[...] = jnp.where(lane == 0, own, 0.0)


def swap(x, name, step):
    size = lax.axis_size(name)
    return lax.ppermute(x, name, [(i, i ^ step) for i in range(size)])


def on_device(alm, beam, m_table, chan_mask, noise):
    ma, pol, freq = (lax.axis_index(name) for name in ("ma", "pol", "freq"))
    n_ma, n_pol, n_freq = (lax.axis_size(name) for name in ("ma", "pol", "freq"))
    parts, _, ell, _, maps = alm.shape
    modes = beam.shape[3]
    place = jnp.stack(
        [ma, pol, m_table[0], jnp.int32(n_pol), ma * n_pol + pol, freq]
    ).astype(jnp.int32)
    flat = alm[:, 0]
    response = beam[0, 0]

    def slab(step):
        return lax.dynamic_index_in_dim(flat, ma ^ step, axis=2, keepdims=False)

    arrived = {}
    for step in (3, 2, 1):
        arrived[step] = swap(slab(step), "ma", step)
    arrived[0] = slab(0)
    near = [arrived[0], swap(arrived[0], "pol", 1), arrived[1], swap(arrived[1], "pol", 1)]
    far = [arrived[3], arrived[2], swap(arrived[3], "pol", 1), swap(arrived[2], "pol", 1)]
    near_steps = ((0, 0), (0, 1), (1, 0), (1, 1))
    far_steps = ((3, 0), (2, 0), (3, 1), (2, 1))
    vis_shape = jax.ShapeDtypeStruct((parts, modes, maps), jnp.float32)
    row = jax.ShapeDtypeStruct((8, 128), jnp.float32)
    params = pltpu.CompilerParams(vmem_limit_bytes=40 << 20)
    flops = 2 * 4 * modes * maps * ell * 4
    early = pl.pallas_call(
        functools.partial(early_kernel, near_steps),
        out_shape=vis_shape,
        in_specs=[SMEM, VMEM] + [VMEM] * 4,
        out_specs=VMEM,
        compiler_params=params,
        cost_estimate=pl.CostEstimate(flops=flops, bytes_accessed=5 << 20, transcendentals=0),
        name="early",
    )(place, response, *near)
    vis, power = pl.pallas_call(
        functools.partial(late_kernel, far_steps, n_freq),
        out_shape=(vis_shape, row),
        in_specs=[SMEM, SMEM] + [VMEM] * 3 + [VMEM] * 4,
        out_specs=(VMEM, VMEM),
        compiler_params=params,
        cost_estimate=pl.CostEstimate(flops=flops, bytes_accessed=7 << 20, transcendentals=0),
        name="late",
    )(place, chan_mask, response, noise, early, *far)
    total = power
    for name in ("pol", "freq", "ma"):
        step = 1
        while step < lax.axis_size(name):
            total = total + swap(total, name, step)
            step *= 2
    scaled, own = pl.pallas_call(
        functools.partial(finish_kernel, n_freq, n_ma * n_pol * modes * maps),
        out_shape=(
            jax.ShapeDtypeStruct((parts, modes, maps), jnp.bfloat16),
            jax.ShapeDtypeStruct((1, 128), jnp.float32),
        ),
        in_specs=[SMEM, SMEM] + [VMEM] * 3,
        out_specs=(VMEM, VMEM),
        compiler_params=params,
        cost_estimate=pl.CostEstimate(flops=1 << 20, bytes_accessed=3 << 20, transcendentals=0),
        name="finish",
    )(place, chan_mask, noise, total, vis)
    return scaled[:, None, None], own[0, :1]


def on_device_plain(alm, beam, m_table, chan_mask, noise):
    arrived = lax.all_to_all(alm, "ma", split_axis=3, concat_axis=2, tiled=True)
    blocks = arrived.reshape(
        arrived.shape[0],
        arrived.shape[1],
        lax.axis_size("ma"),
        arrived.shape[2] // lax.axis_size("ma"),
        arrived.shape[4],
    )
    joined = lax.all_gather(blocks, "pol", axis=3, tiled=True)
    coeffs_all = joined.reshape(
        joined.shape[0], joined.shape[1], joined.shape[2] * joined.shape[3], joined.shape[4]
    )
    degree = lax.iota(jnp.int32, coeffs_all.shape[2])
    keep_mask = (degree >= m_table[0])[None, None, :, None]
    coeffs = jnp.where(keep_mask, coeffs_all, jnp.zeros((), coeffs_all.dtype))
    response = beam[0]
    real_part = jnp.einsum(
        "fkl,fls->fks", response[:, 0], coeffs[0], preferred_element_type=jnp.float32
    ) - jnp.einsum("fkl,fls->fks", response[:, 1], coeffs[1], preferred_element_type=jnp.float32)
    imag_part = jnp.einsum(
        "fkl,fls->fks", response[:, 0], coeffs[1], preferred_element_type=jnp.float32
    ) + jnp.einsum("fkl,fls->fks", response[:, 1], coeffs[0], preferred_element_type=jnp.float32)
    visibility = jnp.stack([real_part, imag_part])
    weighted = visibility * visibility / noise[None, :, :, None]
    partial_power = jnp.sum(weighted, axis=(0, 2, 3))
    modes_total = jnp.float32(
        lax.axis_size("ma") * noise.shape[1] * lax.axis_size("pol") * visibility.shape[3]
    )
    mask_float = chan_mask.astype(jnp.float32)
    channel_power = lax.psum(partial_power, ("ma", "pol")) / modes_total
    masked_sum, live_count = lax.psum(
        (jnp.sum(mask_float * channel_power), jnp.sum(mask_float)), "freq"
    )
    band_power = masked_sum / live_count
    factor = mask_float / jnp.sqrt(0.5 * channel_power + 0.5 * band_power + 1e-06)
    scaled = visibility * (lax.rsqrt(noise) * factor[:, None])[None, :, :, None]
    return (scaled[:, :, None].astype(jnp.bfloat16), channel_power)


def step(alm, beam, m_table, chan_mask, noise):
    aligned = alm.shape[2] % 128 == 0 and lax.axis_size("ma") == 4
    body = on_device if aligned else on_device_plain
    return body(alm, beam, m_table, chan_mask, noise)


def solution(mesh):
    return jax.shard_map(
        step,
        mesh=mesh,
        in_specs=(
            P(None, "freq", ("ma", "pol"), None, "sky"),
            P("ma", "freq", None, "pol", None),
            P("ma"),
            P("freq"),
            P("freq", "pol"),
        ),
        out_specs=(P(None, "freq", "ma", "pol", "sky"), P(("sky", "freq"))),
        check_vma=False,
    )
```

```python
import functools

import jax
import jax.numpy as jnp
from jax import lax
from jax.experimental import pallas as pl
from jax.experimental.pallas import tpu as pltpu
from jax.sharding import PartitionSpec as P

VMEM = pl.BlockSpec(memory_space=pltpu.VMEM)
SMEM = pl.BlockSpec(memory_space=pltpu.SMEM)


def column(row):
    return jnp.transpose(jnp.broadcast_to(row, (128, row.shape[1])))


def split_kernel(steps, alm_ref, *refs):
    *slab_refs, modes_ref = refs
    place = lax.axis_index("ma")
    for c in range(alm_ref.shape[0]):
        modes_ref[...] = pltpu.einshape("lms->mls", alm_ref[c])
        for ref, step in zip(slab_refs, steps, strict=True):
            ref[c] = modes_ref[place ^ step]


def contract(m_ref, beam_ref, block_refs, steps):
    ell = block_refs[0].shape[1]
    left, right_real, right_imag = [], [], []
    for ref, (step, other) in zip(block_refs, steps, strict=True):
        owner = lax.axis_index("ma") ^ step
        half = lax.axis_index("pol") ^ other
        start = (owner * lax.axis_size("pol") + half) * ell
        columns = pl.ds(pl.multiple_of(start, ell), ell)
        degree = start + lax.broadcasted_iota(jnp.int32, (ell, ref.shape[2]), 0)
        keep = degree >= m_ref[0]
        real = jnp.where(keep, ref[0], jnp.zeros((), ref.dtype))
        imag = jnp.where(keep, ref[1], jnp.zeros((), ref.dtype))
        left += [beam_ref[0, :, columns], beam_ref[1, :, columns]]
        right_real += [real, -imag]
        right_imag += [imag, real]
    left = jnp.concatenate(left, axis=1)
    dot = functools.partial(jnp.dot, preferred_element_type=jnp.float32)
    return (
        dot(left, jnp.concatenate(right_real, axis=0)),
        dot(left, jnp.concatenate(right_imag, axis=0)),
    )


def first_kernel(steps, m_ref, mask_ref, beam_ref, *refs):
    *blocks, vis_ref = refs
    vis_ref[0], vis_ref[1] = contract(m_ref, beam_ref, blocks, steps)


def next_kernel(steps, m_ref, beam_ref, before_ref, *refs):
    *blocks, vis_ref = refs
    real, imag = contract(m_ref, beam_ref, blocks, steps)
    vis_ref[0] = real + before_ref[0]
    vis_ref[1] = imag + before_ref[1]


def last_kernel(steps, slots, m_ref, mask_ref, beam_ref, noise_ref, before_ref, *refs):
    *blocks, vis_ref, power_ref = refs
    real, imag = contract(m_ref, beam_ref, blocks, steps)
    real += before_ref[0]
    imag += before_ref[1]
    vis_ref[0] = real
    vis_ref[1] = imag
    squares = real * real + imag * imag
    folded = functools.reduce(
        jnp.add, [squares[:, i : i + 128] for i in range(0, squares.shape[1], 128)]
    )
    total = jnp.sum(folded / column(noise_ref[...]))
    lane = lax.broadcasted_iota(jnp.int32, power_ref.shape, 1)
    leader = (lax.axis_index("ma") == 0) & (lax.axis_index("pol") == 0)
    live = jnp.where(leader, mask_ref[0], 0).astype(jnp.float32)
    channel = lax.axis_index("freq")
    power_ref[...] = jnp.where(lane == channel, total, 0.0) + jnp.where(
        lane == channel + slots, live, 0.0
    )


def finish_kernel(slots, modes, mask_ref, noise_ref, total_ref, vis_ref, scaled_ref, power_ref, held_ref, sems):
    lane = lax.broadcasted_iota(jnp.int32, (1, 128), 1)
    totals = total_ref[0:1, :]
    powers = totals / modes
    live = jnp.sum(jnp.where((lane >= slots) & (lane < 2 * slots), totals, 0.0))
    masks = pltpu.roll(totals, 128 - slots, 1)
    band = jnp.sum(jnp.where(lane < slots, powers * masks, 0.0))
    own = jnp.sum(jnp.where(lane == lax.axis_index("freq"), powers, 0.0))
    mask = mask_ref[0].astype(jnp.float32)
    inner = jnp.full((1, noise_ref.shape[1]), 0.5 * own + 1e-06, jnp.float32)
    inner += 0.5 * (jnp.full_like(inner, band) / jnp.full_like(inner, live))
    factor = mask / jnp.sqrt(inner)
    scale = column(lax.rsqrt(noise_ref[...]) * factor)
    copies = []
    parts, rows, maps = vis_ref.shape
    chunk = rows // 2
    for c in range(parts):
        for j in range(2):
            band_rows = pl.ds(j * chunk, chunk)
            for i in range(0, maps, 128):
                held_ref[c, band_rows, i : i + 128] = (
                    vis_ref[c, band_rows, i : i + 128] * scale[j * chunk : (j + 1) * chunk]
                ).astype(scaled_ref.dtype)
            copies.append(
                pltpu.make_async_copy(
                    held_ref.at[c, band_rows], scaled_ref.at[c, band_rows], sems.at[len(copies)]
                )
            )
            copies[-1].start()
    power_ref[...] = jnp.where(lane == 0, own, 0.0)
    for copy in copies:
        copy.wait()


def swap(x, name, step):
    size = lax.axis_size(name)
    return lax.ppermute(x, name, [(i, i ^ step) for i in range(size)])


def on_device(alm, beam, m_table, chan_mask, noise):
    n_ma, n_pol, n_freq = (lax.axis_size(name) for name in ("ma", "pol", "freq"))
    parts, _, ell, _, maps = alm.shape
    modes = beam.shape[3]
    response = beam[0, 0]
    params = pltpu.CompilerParams(vmem_limit_bytes=40 << 20)
    vis_shape = jax.ShapeDtypeStruct((parts, modes, maps), jnp.float32)
    slab = jax.ShapeDtypeStruct((parts, ell, maps), alm.dtype)

    def cost(blocks, extra):
        return pl.CostEstimate(
            flops=blocks * 2 * 4 * modes * maps * ell,
            bytes_accessed=blocks * (parts * ell * (maps + modes) * 2) + extra,
            transcendentals=0,
        )

    order = (3, 2, 1, 0)
    slabs = pl.pallas_call(
        functools.partial(split_kernel, order),
        out_shape=[slab] * n_ma,
        in_specs=[VMEM],
        out_specs=[VMEM] * n_ma,
        scratch_shapes=[pltpu.VMEM((n_ma, ell, maps), alm.dtype)],
        compiler_params=params,
        cost_estimate=pl.CostEstimate(flops=0, bytes_accessed=4 << 20, transcendentals=0),
        name="split",
    )(alm[:, 0])
    three, two, one, own = slabs
    three = swap(three, "ma", 3)
    two = swap(two, "ma", 2)
    one = swap(one, "ma", 1)
    near = [own, swap(own, "pol", 1), one, swap(one, "pol", 1)]
    vis = pl.pallas_call(
        functools.partial(first_kernel, ((0, 0), (0, 1), (1, 0), (1, 1))),
        out_shape=vis_shape,
        in_specs=[SMEM, SMEM] + [VMEM] * 5,
        out_specs=VMEM,
        compiler_params=params,
        cost_estimate=cost(4, 2 << 20),
        name="first",
    )(m_table, chan_mask, response, *near)
    three_far, two_far = swap(three, "pol", 1), swap(two, "pol", 1)
    vis = pl.pallas_call(
        functools.partial(next_kernel, ((3, 0), (2, 0))),
        out_shape=vis_shape,
        in_specs=[SMEM] + [VMEM] * 4,
        out_specs=VMEM,
        compiler_params=params,
        cost_estimate=cost(2, 4 << 20),
        name="next",
    )(m_table, response, vis, three, two)
    vis, power = pl.pallas_call(
        functools.partial(last_kernel, ((3, 1), (2, 1)), n_freq),
        out_shape=(vis_shape, jax.ShapeDtypeStruct((8, 128), jnp.float32)),
        in_specs=[SMEM, SMEM] + [VMEM] * 5,
        out_specs=(VMEM, VMEM),
        compiler_params=params,
        cost_estimate=cost(2, 4 << 20),
        name="last",
    )(m_table, chan_mask, response, noise, vis, three_far, two_far)
    total = power
    for name in ("pol", "freq", "ma"):
        step = 1
        while step < lax.axis_size(name):
            total = total + swap(total, name, step)
            step *= 2
    scaled, own_power = pl.pallas_call(
        functools.partial(finish_kernel, n_freq, n_ma * n_pol * modes * maps),
        out_shape=(
            jax.ShapeDtypeStruct((parts, modes, maps), jnp.bfloat16),
            jax.ShapeDtypeStruct((1, 128), jnp.float32),
        ),
        in_specs=[SMEM] + [VMEM] * 3,
        out_specs=(pl.BlockSpec(memory_space=pltpu.HBM), VMEM),
        scratch_shapes=[
            pltpu.VMEM((parts, modes, maps), jnp.bfloat16),
            pltpu.SemaphoreType.DMA((2 * parts,)),
        ],
        compiler_params=params,
        cost_estimate=pl.CostEstimate(flops=1 << 20, bytes_accessed=3 << 20, transcendentals=0),
        name="finish",
    )(chan_mask, noise, total, vis)
    return scaled[:, None, None], own_power[0, :1]


def on_device_plain(alm, beam, m_table, chan_mask, noise):
    arrived = lax.all_to_all(alm, "ma", split_axis=3, concat_axis=2, tiled=True)
    blocks = arrived.reshape(
        arrived.shape[0],
        arrived.shape[1],
        lax.axis_size("ma"),
        arrived.shape[2] // lax.axis_size("ma"),
        arrived.shape[4],
    )
    joined = lax.all_gather(blocks, "pol", axis=3, tiled=True)
    coeffs_all = joined.reshape(
        joined.shape[0], joined.shape[1], joined.shape[2] * joined.shape[3], joined.shape[4]
    )
    degree = lax.iota(jnp.int32, coeffs_all.shape[2])
    keep_mask = (degree >= m_table[0])[None, None, :, None]
    coeffs = jnp.where(keep_mask, coeffs_all, jnp.zeros((), coeffs_all.dtype))
    response = beam[0]
    real_part = jnp.einsum(
        "fkl,fls->fks", response[:, 0], coeffs[0], preferred_element_type=jnp.float32
    ) - jnp.einsum("fkl,fls->fks", response[:, 1], coeffs[1], preferred_element_type=jnp.float32)
    imag_part = jnp.einsum(
        "fkl,fls->fks", response[:, 0], coeffs[1], preferred_element_type=jnp.float32
    ) + jnp.einsum("fkl,fls->fks", response[:, 1], coeffs[0], preferred_element_type=jnp.float32)
    visibility = jnp.stack([real_part, imag_part])
    weighted = visibility * visibility / noise[None, :, :, None]
    partial_power = jnp.sum(weighted, axis=(0, 2, 3))
    modes_total = jnp.float32(
        lax.axis_size("ma") * noise.shape[1] * lax.axis_size("pol") * visibility.shape[3]
    )
    mask_float = chan_mask.astype(jnp.float32)
    channel_power = lax.psum(partial_power, ("ma", "pol")) / modes_total
    masked_sum, live_count = lax.psum(
        (jnp.sum(mask_float * channel_power), jnp.sum(mask_float)), "freq"
    )
    band_power = masked_sum / live_count
    factor = mask_float / jnp.sqrt(0.5 * channel_power + 0.5 * band_power + 1e-06)
    scaled = visibility * (lax.rsqrt(noise) * factor[:, None])[None, :, :, None]
    return (scaled[:, :, None].astype(jnp.bfloat16), channel_power)


def step(alm, beam, m_table, chan_mask, noise):
    if alm.shape[2] % 128 == 0 and lax.axis_size("ma") == 4:
        return on_device(alm, beam, m_table, chan_mask, noise)
    return on_device_plain(alm, beam, m_table, chan_mask, noise)


def solution(mesh):
    return jax.shard_map(
        step,
        mesh=mesh,
        in_specs=(
            P(None, "freq", ("ma", "pol"), None, "sky"),
            P("ma", "freq", None, "pol", None),
            P("ma"),
            P("freq"),
            P("freq", "pol"),
        ),
        out_specs=(P(None, "freq", "ma", "pol", "sky"), P(("sky", "freq"))),
        check_vma=False,
    )
```

```python
import functools

import jax
import jax.numpy as jnp
from jax import lax
from jax.experimental import pallas as pl
from jax.experimental.pallas import tpu as pltpu
from jax.sharding import PartitionSpec as P

VMEM = pl.BlockSpec(memory_space=pltpu.VMEM)
SMEM = pl.BlockSpec(memory_space=pltpu.SMEM)


def column(row):
    return jnp.transpose(jnp.broadcast_to(row, (128, row.shape[1])))


def split_kernel(steps, alm_ref, *refs):
    *slab_refs, modes_ref = refs
    place = lax.axis_index("ma")
    for c in range(alm_ref.shape[0]):
        modes_ref[...] = pltpu.einshape("lms->mls", alm_ref[c])
        for ref, step in zip(slab_refs, steps, strict=True):
            ref[c] = modes_ref[place ^ step]


def contract(m_ref, beam_ref, block_refs, steps):
    ell = block_refs[0].shape[1]
    left, right_real, right_imag = [], [], []
    for ref, (step, other) in zip(block_refs, steps, strict=True):
        owner = lax.axis_index("ma") ^ step
        half = lax.axis_index("pol") ^ other
        start = (owner * lax.axis_size("pol") + half) * ell
        columns = pl.ds(pl.multiple_of(start, ell), ell)
        degree = start + lax.broadcasted_iota(jnp.int32, (ell, ref.shape[2]), 0)
        keep = degree >= m_ref[0]
        real = jnp.where(keep, ref[0], jnp.zeros((), ref.dtype))
        imag = jnp.where(keep, ref[1], jnp.zeros((), ref.dtype))
        left += [beam_ref[0, :, columns], beam_ref[1, :, columns]]
        right_real += [real, -imag]
        right_imag += [imag, real]
    left = jnp.concatenate(left, axis=1)
    dot = functools.partial(jnp.dot, preferred_element_type=jnp.float32)
    return (
        dot(left, jnp.concatenate(right_real, axis=0)),
        dot(left, jnp.concatenate(right_imag, axis=0)),
    )


def first_kernel(steps, m_ref, mask_ref, beam_ref, noise_ref, *refs):
    *blocks, vis_ref, weight_ref = refs
    vis_ref[0], vis_ref[1] = contract(m_ref, beam_ref, blocks, steps)
    weight_ref[...] = column(lax.rsqrt(noise_ref[...]))


def at_edge():
    place = lax.axis_index("ma")
    return (place == 0) | (place == lax.axis_size("ma") - 1)


def weigh(vis, weight):
    return jnp.concatenate(
        [vis[:, i : i + 128] * weight for i in range(0, vis.shape[1], 128)], axis=1
    )


def power_of(real, imag):
    squares = real * real + imag * imag
    folded = functools.reduce(
        jnp.add, [squares[:, i : i + 128] for i in range(0, squares.shape[1], 128)]
    )
    return jnp.sum(folded)


def edge_kernel(steps, m_ref, beam_ref, weight_ref, before_ref, *refs):
    *blocks, vis_ref, power_ref = refs
    real, imag = contract(m_ref, beam_ref, blocks, steps)
    real += before_ref[0]
    imag += before_ref[1]
    vis_ref[0] = real
    vis_ref[1] = imag
    weight = weight_ref[...]
    total = power_of(weigh(real, weight), weigh(imag, weight))
    lane = lax.broadcasted_iota(jnp.int32, power_ref.shape, 1)
    here = (lane == lax.axis_index("freq")) & at_edge()
    power_ref[...] = jnp.where(here, total, 0.0)


def next_kernel(steps, m_ref, beam_ref, before_ref, *refs):
    *blocks, vis_ref = refs
    real, imag = contract(m_ref, beam_ref, blocks, steps)
    vis_ref[0] = real + before_ref[0]
    vis_ref[1] = imag + before_ref[1]


def live_kernel(slots, mask_ref, live_ref):
    lane = lax.broadcasted_iota(jnp.int32, live_ref.shape, 1)
    leader = (lax.axis_index("ma") == 1) & (lax.axis_index("pol") == 0)
    here = (lane == lax.axis_index("freq") + slots) & leader
    live_ref[...] = jnp.where(here, mask_ref[0].astype(jnp.float32), 0.0)


def last_kernel(steps, m_ref, beam_ref, weight_ref, before_ref, *refs):
    *blocks, edge_ref, live_ref, vis_ref, power_ref = refs
    real, imag = contract(m_ref, beam_ref, blocks, steps)
    weight = weight_ref[...]
    real = weigh(real + before_ref[0], weight)
    imag = weigh(imag + before_ref[1], weight)
    vis_ref[0] = real
    vis_ref[1] = imag
    total = power_of(real, imag)
    lane = lax.broadcasted_iota(jnp.int32, power_ref.shape, 1)
    here = (lane == lax.axis_index("freq")) & jnp.logical_not(at_edge())
    power_ref[...] = jnp.where(here, total, 0.0) + edge_ref[...] + live_ref[...]


def finish_kernel(slots, modes, mask_ref, total_ref, vis_ref, scaled_ref, power_ref, held_ref, sems):
    lane = lax.broadcasted_iota(jnp.int32, (1, 128), 1)
    totals = total_ref[0:1, :]
    powers = totals / modes
    masks = pltpu.roll(totals, 128 - slots, 1)

    def over(where, values):
        return jnp.sum(jnp.where(where, values, 0.0), axis=1, keepdims=True)

    band = over(lane < slots, powers * masks) / over(lane < slots, masks)
    own = over(lane == lax.axis_index("freq"), powers)
    mask = mask_ref[0].astype(jnp.float32)
    factor = mask / jnp.sqrt(0.5 * own + 0.5 * band + 1e-06)
    power_ref[...] = jnp.where(lane == 0, own, 0.0)
    copies = []
    parts, rows, _ = vis_ref.shape
    chunk = rows // 4
    for c in range(parts):
        for j in range(0, rows, chunk):
            held_ref[c, j : j + chunk] = (vis_ref[c, j : j + chunk] * factor).astype(
                scaled_ref.dtype
            )
            copies.append(
                pltpu.make_async_copy(
                    held_ref.at[c, pl.ds(j, chunk)],
                    scaled_ref.at[c, pl.ds(j, chunk)],
                    sems.at[len(copies)],
                )
            )
            copies[-1].start()
    for copy in copies:
        copy.wait()


def swap(x, name, step):
    return lax.ppermute(x, name, [(i, i ^ step) for i in range(lax.axis_size(name))])


def on_device(alm, beam, m_table, chan_mask, noise):
    n_ma, n_pol, n_freq = (lax.axis_size(name) for name in ("ma", "pol", "freq"))
    parts, _, ell, _, maps = alm.shape
    modes = beam.shape[3]
    response = beam[0, 0]
    params = pltpu.CompilerParams(vmem_limit_bytes=24 << 20)
    vis_shape = jax.ShapeDtypeStruct((parts, modes, maps), jnp.float32)
    slab = jax.ShapeDtypeStruct((parts, ell, maps), alm.dtype)
    row = jax.ShapeDtypeStruct((8, 128), jnp.float32)
    weights = jax.ShapeDtypeStruct((modes, 128), jnp.float32)

    def call(kernel, out_shape, scalars, operands, blocks, **more):
        return pl.pallas_call(
            kernel,
            out_shape=out_shape,
            in_specs=[SMEM] * len(scalars) + [VMEM] * len(operands),
            out_specs=more.pop("out_specs", jax.tree.map(lambda _: VMEM, out_shape)),
            compiler_params=params,
            cost_estimate=pl.CostEstimate(
                flops=blocks * 2 * 4 * modes * maps * ell,
                bytes_accessed=(blocks + 4) * parts * ell * (maps + modes) * 2,
                transcendentals=0,
            ),
            **more,
        )(*scalars, *operands)

    two, one, three, own = call(
        functools.partial(split_kernel, (2, 1, 3, 0)),
        [slab] * n_ma,
        (),
        (alm[:, 0],),
        0,
        scratch_shapes=[pltpu.VMEM((n_ma, ell, maps), alm.dtype)],
    )
    two = swap(two, "ma", 2)
    one = swap(one, "ma", 1)
    edge = lax.ppermute(three, "ma", [(0, 3), (3, 0)])
    middle = lax.ppermute(three, "ma", [(1, 2), (2, 1)])
    own_far = swap(own, "pol", 1)
    one_far = swap(one, "pol", 1)
    two_far = swap(two, "pol", 1)
    edge_far = swap(edge, "pol", 1)
    middle_far = swap(middle, "pol", 1)
    steps = ((0, 0), (0, 1), (1, 0), (1, 1), (2, 0), (2, 1))
    vis, weight = call(
        functools.partial(first_kernel, steps),
        (vis_shape, weights),
        (m_table, chan_mask),
        (response, noise, own, own_far, one, one_far, two, two_far),
        6,
    )
    vis, edge_power = call(
        functools.partial(edge_kernel, ((3, 0), (3, 1))),
        (vis_shape, row),
        (m_table,),
        (response, weight, vis, edge, edge_far),
        2,
    )
    edge_power = lax.ppermute(edge_power, "ma", [(0, 1), (3, 2)])
    live = call(functools.partial(live_kernel, n_freq), row, (chan_mask,), (), 0)
    vis = call(
        functools.partial(next_kernel, ((3, 0),)), vis_shape, (m_table,), (response, vis, middle), 1
    )
    vis, total = call(
        functools.partial(last_kernel, ((3, 1),)),
        (vis_shape, row),
        (m_table,),
        (response, weight, vis, middle_far, edge_power, live),
        1,
    )
    total += swap(total, "pol", 1)
    total += swap(total, "freq", 1)
    beyond = lax.ppermute(total, "ma", [(1, 3), (2, 0)])
    beside = lax.ppermute(total, "ma", [(1, 0), (2, 3)])
    across = lax.ppermute(total, "ma", [(1, 2), (2, 1)])
    total = total + beyond + beside + across
    scaled, own_power = call(
        functools.partial(finish_kernel, n_freq, n_ma * n_pol * modes * maps),
        (
            jax.ShapeDtypeStruct((parts, modes, maps), jnp.bfloat16),
            jax.ShapeDtypeStruct((1, 128), jnp.float32),
        ),
        (chan_mask,),
        (total, vis),
        0,
        out_specs=(pl.BlockSpec(memory_space=pltpu.HBM), VMEM),
        scratch_shapes=[
            pltpu.VMEM((parts, modes, maps), jnp.bfloat16),
            pltpu.SemaphoreType.DMA((4 * parts,)),
        ],
    )
    return scaled[:, None, None], own_power[0, :1]


def on_device_plain(alm, beam, m_table, chan_mask, noise):
    arrived = lax.all_to_all(alm, "ma", split_axis=3, concat_axis=2, tiled=True)
    blocks = arrived.reshape(
        arrived.shape[0],
        arrived.shape[1],
        lax.axis_size("ma"),
        arrived.shape[2] // lax.axis_size("ma"),
        arrived.shape[4],
    )
    joined = lax.all_gather(blocks, "pol", axis=3, tiled=True)
    coeffs_all = joined.reshape(
        joined.shape[0], joined.shape[1], joined.shape[2] * joined.shape[3], joined.shape[4]
    )
    degree = lax.iota(jnp.int32, coeffs_all.shape[2])
    keep_mask = (degree >= m_table[0])[None, None, :, None]
    coeffs = jnp.where(keep_mask, coeffs_all, jnp.zeros((), coeffs_all.dtype))
    response = beam[0]
    real_part = jnp.einsum(
        "fkl,fls->fks", response[:, 0], coeffs[0], preferred_element_type=jnp.float32
    ) - jnp.einsum("fkl,fls->fks", response[:, 1], coeffs[1], preferred_element_type=jnp.float32)
    imag_part = jnp.einsum(
        "fkl,fls->fks", response[:, 0], coeffs[1], preferred_element_type=jnp.float32
    ) + jnp.einsum("fkl,fls->fks", response[:, 1], coeffs[0], preferred_element_type=jnp.float32)
    visibility = jnp.stack([real_part, imag_part])
    weighted = visibility * visibility / noise[None, :, :, None]
    partial_power = jnp.sum(weighted, axis=(0, 2, 3))
    modes_total = jnp.float32(
        lax.axis_size("ma") * noise.shape[1] * lax.axis_size("pol") * visibility.shape[3]
    )
    mask_float = chan_mask.astype(jnp.float32)
    channel_power = lax.psum(partial_power, ("ma", "pol")) / modes_total
    masked_sum, live_count = lax.psum(
        (jnp.sum(mask_float * channel_power), jnp.sum(mask_float)), "freq"
    )
    band_power = masked_sum / live_count
    factor = mask_float / jnp.sqrt(0.5 * channel_power + 0.5 * band_power + 1e-06)
    scaled = visibility * (lax.rsqrt(noise) * factor[:, None])[None, :, :, None]
    return (scaled[:, :, None].astype(jnp.bfloat16), channel_power)


def step(alm, beam, m_table, chan_mask, noise):
    sizes = [lax.axis_size(name) for name in ("ma", "freq", "pol")]
    if alm.shape[2] % 128 == 0 and sizes == [4, 2, 2]:
        return on_device(alm, beam, m_table, chan_mask, noise)
    return on_device_plain(alm, beam, m_table, chan_mask, noise)


def solution(mesh):
    return jax.shard_map(
        step,
        mesh=mesh,
        in_specs=(
            P(None, "freq", ("ma", "pol"), None, "sky"),
            P("ma", "freq", None, "pol", None),
            P("ma"),
            P("freq"),
            P("freq", "pol"),
        ),
        out_specs=(P(None, "freq", "ma", "pol", "sky"), P(("sky", "freq"))),
        check_vma=False,
    )
```

```python
import functools

import jax
import jax.numpy as jnp
from jax import lax
from jax.experimental import pallas as pl
from jax.experimental.pallas import tpu as pltpu
from jax.sharding import PartitionSpec as P

VMEM = pl.BlockSpec(memory_space=pltpu.VMEM)
SMEM = pl.BlockSpec(memory_space=pltpu.SMEM)
HBM = pl.BlockSpec(memory_space=pltpu.HBM)


def column(row):
    return jnp.transpose(jnp.broadcast_to(row, (128, row.shape[1])))


def split_kernel(steps, alm_ref, *refs):
    *slab_refs, modes_ref = refs
    place = lax.axis_index("ma")
    for c in range(alm_ref.shape[0]):
        modes_ref[...] = pltpu.einshape("lms->mls", alm_ref[c])
        for ref, step in zip(slab_refs, steps, strict=True):
            ref[c] = modes_ref[place ^ step]


def load_kernel(beam_ref, noise_ref, left_ref, weight_ref, sems):
    _, _, total = beam_ref.shape
    blocks = left_ref.shape[0]
    ell = total // blocks
    copies = []
    for block in range(blocks):
        for c in range(2):
            copies.append(
                pltpu.make_async_copy(
                    beam_ref.at[c, :, pl.ds(block * ell, ell)],
                    left_ref.at[block, :, pl.ds(c * ell, ell)],
                    sems.at[2 * block + c],
                )
            )
            copies[-1].start()
    weight_ref[...] = column(lax.rsqrt(noise_ref[...]))
    for copy in copies:
        copy.wait()


def contract(m_ref, left_ref, block_refs, steps):
    ell = block_refs[0].shape[1]
    left, right_real, right_imag = [], [], []
    for ref, (step, other) in zip(block_refs, steps, strict=True):
        owner = lax.axis_index("ma") ^ step
        half = lax.axis_index("pol") ^ other
        block = owner * lax.axis_size("pol") + half
        degree = block * ell + lax.broadcasted_iota(jnp.int32, (ell, ref.shape[2]), 0)
        keep = degree >= m_ref[0]
        real = jnp.where(keep, ref[0], jnp.zeros((), ref.dtype))
        imag = jnp.where(keep, ref[1], jnp.zeros((), ref.dtype))
        left.append(left_ref[block])
        right_real += [real, -imag]
        right_imag += [imag, real]
    left = jnp.concatenate(left, axis=1)
    dot = functools.partial(jnp.dot, preferred_element_type=jnp.float32)
    return (
        dot(left, jnp.concatenate(right_real, axis=0)),
        dot(left, jnp.concatenate(right_imag, axis=0)),
    )


def first_kernel(steps, m_ref, mask_ref, left_ref, *refs):
    del mask_ref
    *blocks, vis_ref = refs
    vis_ref[0], vis_ref[1] = contract(m_ref, left_ref, blocks, steps)


def weigh(vis, weight):
    return jnp.concatenate(
        [vis[:, i : i + 128] * weight for i in range(0, vis.shape[1], 128)], axis=1
    )


def power_of(real, imag):
    squares = real * real + imag * imag
    folded = functools.reduce(
        jnp.add, [squares[:, i : i + 128] for i in range(0, squares.shape[1], 128)]
    )
    return jnp.sum(folded)


def next_kernel(steps, m_ref, left_ref, before_ref, *refs):
    *blocks, vis_ref = refs
    real, imag = contract(m_ref, left_ref, blocks, steps)
    vis_ref[0] = real + before_ref[0]
    vis_ref[1] = imag + before_ref[1]


def last_kernel(steps, slots, m_ref, mask_ref, left_ref, weight_ref, before_ref, *refs):
    *blocks, vis_ref, power_ref = refs
    real, imag = contract(m_ref, left_ref, blocks, steps)
    weight = weight_ref[...]
    real = weigh(real + before_ref[0], weight)
    imag = weigh(imag + before_ref[1], weight)
    vis_ref[0] = real
    vis_ref[1] = imag
    total = power_of(real, imag)
    lane = lax.broadcasted_iota(jnp.int32, power_ref.shape, 1)
    leader = (lax.axis_index("ma") == 0) & (lax.axis_index("pol") == 0)
    live = jnp.where(leader, mask_ref[0], 0).astype(jnp.float32)
    channel = lax.axis_index("freq")
    power_ref[...] = jnp.where(lane == channel, total, 0.0) + jnp.where(
        lane == channel + slots, live, 0.0
    )


def finish_kernel(slots, modes, mask_ref, total_ref, vis_ref, scaled_ref, power_ref, held_ref, own_ref, sems):
    lane = lax.broadcasted_iota(jnp.int32, (1, 128), 1)
    totals = total_ref[0:1, :]
    powers = totals / modes
    masks = pltpu.roll(totals, 128 - slots, 1)

    def over(where, values):
        return jnp.sum(jnp.where(where, values, 0.0), axis=1, keepdims=True)

    band = over(lane < slots, powers * masks) / over(lane < slots, masks)
    own = over(lane == lax.axis_index("freq"), powers)
    mask = mask_ref[0].astype(jnp.float32)
    factor = mask / jnp.sqrt(0.5 * own + 0.5 * band + 1e-06)
    own_ref[...] = jnp.where(lane == 0, own, 0.0)
    copies = [pltpu.make_async_copy(own_ref, power_ref, sems.at[0])]
    copies[0].start()
    parts, rows, _ = vis_ref.shape
    chunk = rows // 4
    for c in range(parts):
        for j in range(0, rows, chunk):
            held_ref[c, j : j + chunk] = (vis_ref[c, j : j + chunk] * factor).astype(
                scaled_ref.dtype
            )
            copies.append(
                pltpu.make_async_copy(
                    held_ref.at[c, pl.ds(j, chunk)],
                    scaled_ref.at[c, pl.ds(j, chunk)],
                    sems.at[len(copies)],
                )
            )
            copies[-1].start()
    for copy in copies:
        copy.wait()


def swap(x, name, step):
    return lax.ppermute(x, name, [(i, i ^ step) for i in range(lax.axis_size(name))])


def on_device(alm, beam, m_table, chan_mask, noise):
    n_ma, n_pol, n_freq = (lax.axis_size(name) for name in ("ma", "pol", "freq"))
    parts, _, ell, _, maps = alm.shape
    modes = beam.shape[3]
    response = beam[0, 0]
    params = pltpu.CompilerParams(vmem_limit_bytes=24 << 20)
    vis_shape = jax.ShapeDtypeStruct((parts, modes, maps), jnp.float32)
    slab = jax.ShapeDtypeStruct((parts, ell, maps), alm.dtype)
    row = jax.ShapeDtypeStruct((8, 128), jnp.float32)
    weights = jax.ShapeDtypeStruct((modes, 128), jnp.float32)

    def call(kernel, out_shape, scalars, operands, blocks, **more):
        return pl.pallas_call(
            kernel,
            out_shape=out_shape,
            in_specs=more.pop("in_specs", [SMEM] * len(scalars) + [VMEM] * len(operands)),
            out_specs=more.pop("out_specs", jax.tree.map(lambda _: VMEM, out_shape)),
            compiler_params=params,
            cost_estimate=pl.CostEstimate(
                flops=blocks * 2 * 4 * modes * maps * ell,
                bytes_accessed=(blocks + 4) * parts * ell * (maps + modes) * 2,
                transcendentals=0,
            ),
            **more,
        )(*scalars, *operands)

    three, one, two, own = call(
        functools.partial(split_kernel, (3, 1, 2, 0)),
        [slab] * n_ma,
        (),
        (alm[:, 0],),
        0,
        scratch_shapes=[pltpu.VMEM((n_ma, ell, maps), alm.dtype)],
    )
    three = swap(three, "ma", 3)
    one = swap(one, "ma", 1)
    two = swap(two, "ma", 2)
    own_far = swap(own, "pol", 1)
    one_far = swap(one, "pol", 1)
    three_far = swap(three, "pol", 1)
    two_far = swap(two, "pol", 1)
    blocks = n_ma * n_pol
    left, weight = call(
        load_kernel,
        (jax.ShapeDtypeStruct((blocks, modes, 2 * ell), beam.dtype), weights),
        (),
        (response, noise),
        0,
        in_specs=[HBM, VMEM],
        scratch_shapes=[pltpu.SemaphoreType.DMA((2 * blocks,))],
    )
    steps = ((0, 0), (0, 1), (1, 0), (1, 1), (3, 0), (3, 1))
    vis = call(
        functools.partial(first_kernel, steps),
        vis_shape,
        (m_table, chan_mask),
        (left, own, own_far, one, one_far, three, three_far),
        6,
    )
    vis = call(
        functools.partial(next_kernel, ((2, 0),)), vis_shape, (m_table,), (left, vis, two), 1
    )
    vis, total = call(
        functools.partial(last_kernel, ((2, 1),), n_freq),
        (vis_shape, row),
        (m_table, chan_mask),
        (left, weight, vis, two_far),
        1,
    )
    for name in ("pol", "freq", "ma"):
        step = 1
        while step < lax.axis_size(name):
            total = total + swap(total, name, step)
            step *= 2
    scaled, own_power = call(
        functools.partial(finish_kernel, n_freq, n_ma * n_pol * modes * maps),
        (
            jax.ShapeDtypeStruct((parts, modes, maps), jnp.bfloat16),
            jax.ShapeDtypeStruct((1, 128), jnp.float32),
        ),
        (chan_mask,),
        (total, vis),
        0,
        out_specs=(HBM, HBM),
        scratch_shapes=[
            pltpu.VMEM((parts, modes, maps), jnp.bfloat16),
            pltpu.VMEM((1, 128), jnp.float32),
            pltpu.SemaphoreType.DMA((4 * parts + 1,)),
        ],
    )
    return scaled[:, None, None], own_power[0, :1]


def on_device_plain(alm, beam, m_table, chan_mask, noise):
    arrived = lax.all_to_all(alm, "ma", split_axis=3, concat_axis=2, tiled=True)
    blocks = arrived.reshape(
        arrived.shape[0],
        arrived.shape[1],
        lax.axis_size("ma"),
        arrived.shape[2] // lax.axis_size("ma"),
        arrived.shape[4],
    )
    joined = lax.all_gather(blocks, "pol", axis=3, tiled=True)
    coeffs_all = joined.reshape(
        joined.shape[0], joined.shape[1], joined.shape[2] * joined.shape[3], joined.shape[4]
    )
    degree = lax.iota(jnp.int32, coeffs_all.shape[2])
    keep_mask = (degree >= m_table[0])[None, None, :, None]
    coeffs = jnp.where(keep_mask, coeffs_all, jnp.zeros((), coeffs_all.dtype))
    response = beam[0]
    real_part = jnp.einsum(
        "fkl,fls->fks", response[:, 0], coeffs[0], preferred_element_type=jnp.float32
    ) - jnp.einsum("fkl,fls->fks", response[:, 1], coeffs[1], preferred_element_type=jnp.float32)
    imag_part = jnp.einsum(
        "fkl,fls->fks", response[:, 0], coeffs[1], preferred_element_type=jnp.float32
    ) + jnp.einsum("fkl,fls->fks", response[:, 1], coeffs[0], preferred_element_type=jnp.float32)
    visibility = jnp.stack([real_part, imag_part])
    weighted = visibility * visibility / noise[None, :, :, None]
    partial_power = jnp.sum(weighted, axis=(0, 2, 3))
    modes_total = jnp.float32(
        lax.axis_size("ma") * noise.shape[1] * lax.axis_size("pol") * visibility.shape[3]
    )
    mask_float = chan_mask.astype(jnp.float32)
    channel_power = lax.psum(partial_power, ("ma", "pol")) / modes_total
    masked_sum, live_count = lax.psum(
        (jnp.sum(mask_float * channel_power), jnp.sum(mask_float)), "freq"
    )
    band_power = masked_sum / live_count
    factor = mask_float / jnp.sqrt(0.5 * channel_power + 0.5 * band_power + 1e-06)
    scaled = visibility * (lax.rsqrt(noise) * factor[:, None])[None, :, :, None]
    return (scaled[:, :, None].astype(jnp.bfloat16), channel_power)


def step(alm, beam, m_table, chan_mask, noise):
    sizes = [lax.axis_size(name) for name in ("ma", "freq", "pol")]
    if alm.shape[2] % 128 == 0 and sizes == [4, 2, 2]:
        return on_device(alm, beam, m_table, chan_mask, noise)
    return on_device_plain(alm, beam, m_table, chan_mask, noise)


def solution(mesh):
    return jax.shard_map(
        step,
        mesh=mesh,
        in_specs=(
            P(None, "freq", ("ma", "pol"), None, "sky"),
            P("ma", "freq", None, "pol", None),
            P("ma"),
            P("freq"),
            P("freq", "pol"),
        ),
        out_specs=(P(None, "freq", "ma", "pol", "sky"), P(("sky", "freq"))),
        check_vma=False,
    )
```

```python
import functools

import jax
import jax.numpy as jnp
from jax import lax
from jax.experimental import pallas as pl
from jax.experimental.pallas import tpu as pltpu
from jax.sharding import PartitionSpec as P

VMEM = pl.BlockSpec(memory_space=pltpu.VMEM)
SMEM = pl.BlockSpec(memory_space=pltpu.SMEM)
HBM = pl.BlockSpec(memory_space=pltpu.HBM)


def column(row):
    return jnp.transpose(jnp.broadcast_to(row, (128, row.shape[1])))


def split_kernel(steps, alm_ref, *refs):
    *slab_refs, modes_ref = refs
    place = lax.axis_index("ma")
    for c in range(alm_ref.shape[0]):
        modes_ref[...] = pltpu.einshape("lms->mls", alm_ref[c])
        for ref, step in zip(slab_refs, steps, strict=True):
            ref[c] = modes_ref[place ^ step]


def load_kernel(beam_ref, noise_ref, left_ref, weight_ref, sems):
    _, _, total = beam_ref.shape
    blocks = left_ref.shape[0]
    ell = total // blocks
    copies = []
    for block in range(blocks):
        for c in range(2):
            copies.append(
                pltpu.make_async_copy(
                    beam_ref.at[c, :, pl.ds(block * ell, ell)],
                    left_ref.at[block, :, pl.ds(c * ell, ell)],
                    sems.at[2 * block + c],
                )
            )
            copies[-1].start()
    weight_ref[...] = column(lax.rsqrt(noise_ref[...]))
    for copy in copies:
        copy.wait()


def contract(m_ref, left_ref, block_refs, steps):
    ell = block_refs[0].shape[1]
    left, right_real, right_imag = [], [], []
    for ref, (step, other) in zip(block_refs, steps, strict=True):
        owner = lax.axis_index("ma") ^ step
        half = lax.axis_index("pol") ^ other
        block = owner * lax.axis_size("pol") + half
        degree = block * ell + lax.broadcasted_iota(jnp.int32, (ell, ref.shape[2]), 0)
        keep = degree >= m_ref[0]
        real = jnp.where(keep, ref[0], jnp.zeros((), ref.dtype))
        imag = jnp.where(keep, ref[1], jnp.zeros((), ref.dtype))
        left.append(left_ref[block])
        right_real += [real, -imag]
        right_imag += [imag, real]
    left = jnp.concatenate(left, axis=1)
    dot = functools.partial(jnp.dot, preferred_element_type=jnp.float32)
    return (
        dot(left, jnp.concatenate(right_real, axis=0)),
        dot(left, jnp.concatenate(right_imag, axis=0)),
    )


def first_kernel(steps, m_ref, mask_ref, left_ref, *refs):
    del mask_ref
    *blocks, vis_ref = refs
    vis_ref[0], vis_ref[1] = contract(m_ref, left_ref, blocks, steps)


def weigh(vis, weight):
    return jnp.concatenate(
        [vis[:, i : i + 128] * weight for i in range(0, vis.shape[1], 128)], axis=1
    )


def power_of(real, imag):
    squares = real * real + imag * imag
    folded = functools.reduce(
        jnp.add, [squares[:, i : i + 128] for i in range(0, squares.shape[1], 128)]
    )
    return jnp.sum(folded)


def next_kernel(steps, m_ref, left_ref, before_ref, *refs):
    *blocks, vis_ref = refs
    real, imag = contract(m_ref, left_ref, blocks, steps)
    vis_ref[0] = real + before_ref[0]
    vis_ref[1] = imag + before_ref[1]


def last_kernel(steps, slots, m_ref, mask_ref, left_ref, weight_ref, before_ref, *refs):
    *blocks, vis_ref, power_ref = refs
    real, imag = contract(m_ref, left_ref, blocks, steps)
    weight = weight_ref[...]
    real = weigh(real + before_ref[0], weight)
    imag = weigh(imag + before_ref[1], weight)
    vis_ref[0] = real
    vis_ref[1] = imag
    total = power_of(real, imag)
    lane = lax.broadcasted_iota(jnp.int32, power_ref.shape, 1)
    leader = (lax.axis_index("ma") == 0) & (lax.axis_index("pol") == 0)
    live = jnp.where(leader, mask_ref[0], 0).astype(jnp.float32)
    channel = lax.axis_index("freq")
    power_ref[...] = jnp.where(lane == channel, total, 0.0) + jnp.where(
        lane == channel + slots, live, 0.0
    )


def finish_kernel(slots, modes, mask_ref, total_ref, vis_ref, scaled_ref, power_ref, held_ref, own_ref, sems):
    lane = lax.broadcasted_iota(jnp.int32, (1, 128), 1)
    totals = total_ref[0:1, :]
    powers = totals / modes
    masks = pltpu.roll(totals, 128 - slots, 1)

    def over(where, values):
        return jnp.sum(jnp.where(where, values, 0.0), axis=1, keepdims=True)

    band = over(lane < slots, powers * masks) / over(lane < slots, masks)
    own = over(lane == lax.axis_index("freq"), powers)
    mask = mask_ref[0].astype(jnp.float32)
    factor = mask / jnp.sqrt(0.5 * own + 0.5 * band + 1e-06)
    own_ref[...] = jnp.where(lane == 0, own, 0.0)
    copies = [pltpu.make_async_copy(own_ref, power_ref, sems.at[0])]
    copies[0].start()
    parts, rows, _ = vis_ref.shape
    chunk = rows // 4
    for c in range(parts):
        for j in range(0, rows, chunk):
            held_ref[c, j : j + chunk] = (vis_ref[c, j : j + chunk] * factor).astype(
                scaled_ref.dtype
            )
            copies.append(
                pltpu.make_async_copy(
                    held_ref.at[c, pl.ds(j, chunk)],
                    scaled_ref.at[c, pl.ds(j, chunk)],
                    sems.at[len(copies)],
                )
            )
            copies[-1].start()
    for copy in copies:
        copy.wait()


def swap(x, name, step):
    names, flip = ("pol", step) if name == "pol" else ((name, "pol"), 2 * step + 1)
    size = lax.axis_size(names)
    return lax.ppermute(x, names, [(i, i ^ flip) for i in range(size)])


def on_device(alm, beam, m_table, chan_mask, noise):
    n_ma, n_pol, n_freq = (lax.axis_size(name) for name in ("ma", "pol", "freq"))
    parts, _, ell, _, maps = alm.shape
    modes = beam.shape[3]
    response = beam[0, 0]
    params = pltpu.CompilerParams(vmem_limit_bytes=24 << 20)
    vis_shape = jax.ShapeDtypeStruct((parts, modes, maps), jnp.float32)
    slab = jax.ShapeDtypeStruct((parts, ell, maps), alm.dtype)
    row = jax.ShapeDtypeStruct((8, 128), jnp.float32)
    weights = jax.ShapeDtypeStruct((modes, 128), jnp.float32)

    def call(kernel, out_shape, scalars, operands, blocks, **more):
        return pl.pallas_call(
            kernel,
            out_shape=out_shape,
            in_specs=more.pop("in_specs", [SMEM] * len(scalars) + [VMEM] * len(operands)),
            out_specs=more.pop("out_specs", jax.tree.map(lambda _: VMEM, out_shape)),
            compiler_params=params,
            cost_estimate=pl.CostEstimate(
                flops=blocks * 2 * 4 * modes * maps * ell,
                bytes_accessed=(blocks + 4) * parts * ell * (maps + modes) * 2,
                transcendentals=0,
            ),
            **more,
        )(*scalars, *operands)

    three, one, two, own = call(
        functools.partial(split_kernel, (3, 1, 2, 0)),
        [slab] * n_ma,
        (),
        (alm[:, 0],),
        0,
        scratch_shapes=[pltpu.VMEM((n_ma, ell, maps), alm.dtype)],
    )
    three = swap(three, "ma", 3)
    one = swap(one, "ma", 1)
    two = swap(two, "ma", 2)
    own_far = swap(own, "pol", 1)
    one_far = swap(one, "pol", 1)
    three_far = swap(three, "pol", 1)
    two_far = swap(two, "pol", 1)
    blocks = n_ma * n_pol
    left, weight = call(
        load_kernel,
        (jax.ShapeDtypeStruct((blocks, modes, 2 * ell), beam.dtype), weights),
        (),
        (response, noise),
        0,
        in_specs=[HBM, VMEM],
        scratch_shapes=[pltpu.SemaphoreType.DMA((2 * blocks,))],
    )
    steps = ((0, 0), (0, 1), (1, 1), (1, 0), (3, 1), (3, 0))
    vis = call(
        functools.partial(first_kernel, steps),
        vis_shape,
        (m_table, chan_mask),
        (left, own, own_far, one, one_far, three, three_far),
        6,
    )
    vis = call(
        functools.partial(next_kernel, ((2, 1),)), vis_shape, (m_table,), (left, vis, two), 1
    )
    vis, total = call(
        functools.partial(last_kernel, ((2, 0),), n_freq),
        (vis_shape, row),
        (m_table, chan_mask),
        (left, weight, vis, two_far),
        1,
    )
    for name in ("pol", "freq", "ma"):
        step = 1
        while step < lax.axis_size(name):
            total = total + swap(total, name, step)
            step *= 2
    scaled, own_power = call(
        functools.partial(finish_kernel, n_freq, n_ma * n_pol * modes * maps),
        (
            jax.ShapeDtypeStruct((parts, modes, maps), jnp.bfloat16),
            jax.ShapeDtypeStruct((1, 128), jnp.float32),
        ),
        (chan_mask,),
        (total, vis),
        0,
        out_specs=(HBM, HBM),
        scratch_shapes=[
            pltpu.VMEM((parts, modes, maps), jnp.bfloat16),
            pltpu.VMEM((1, 128), jnp.float32),
            pltpu.SemaphoreType.DMA((4 * parts + 1,)),
        ],
    )
    return scaled[:, None, None], own_power[0, :1]


def on_device_plain(alm, beam, m_table, chan_mask, noise):
    arrived = lax.all_to_all(alm, "ma", split_axis=3, concat_axis=2, tiled=True)
    blocks = arrived.reshape(
        arrived.shape[0],
        arrived.shape[1],
        lax.axis_size("ma"),
        arrived.shape[2] // lax.axis_size("ma"),
        arrived.shape[4],
    )
    joined = lax.all_gather(blocks, "pol", axis=3, tiled=True)
    coeffs_all = joined.reshape(
        joined.shape[0], joined.shape[1], joined.shape[2] * joined.shape[3], joined.shape[4]
    )
    degree = lax.iota(jnp.int32, coeffs_all.shape[2])
    keep_mask = (degree >= m_table[0])[None, None, :, None]
    coeffs = jnp.where(keep_mask, coeffs_all, jnp.zeros((), coeffs_all.dtype))
    response = beam[0]
    real_part = jnp.einsum(
        "fkl,fls->fks", response[:, 0], coeffs[0], preferred_element_type=jnp.float32
    ) - jnp.einsum("fkl,fls->fks", response[:, 1], coeffs[1], preferred_element_type=jnp.float32)
    imag_part = jnp.einsum(
        "fkl,fls->fks", response[:, 0], coeffs[1], preferred_element_type=jnp.float32
    ) + jnp.einsum("fkl,fls->fks", response[:, 1], coeffs[0], preferred_element_type=jnp.float32)
    visibility = jnp.stack([real_part, imag_part])
    weighted = visibility * visibility / noise[None, :, :, None]
    partial_power = jnp.sum(weighted, axis=(0, 2, 3))
    modes_total = jnp.float32(
        lax.axis_size("ma") * noise.shape[1] * lax.axis_size("pol") * visibility.shape[3]
    )
    mask_float = chan_mask.astype(jnp.float32)
    channel_power = lax.psum(partial_power, ("ma", "pol")) / modes_total
    masked_sum, live_count = lax.psum(
        (jnp.sum(mask_float * channel_power), jnp.sum(mask_float)), "freq"
    )
    band_power = masked_sum / live_count
    factor = mask_float / jnp.sqrt(0.5 * channel_power + 0.5 * band_power + 1e-06)
    scaled = visibility * (lax.rsqrt(noise) * factor[:, None])[None, :, :, None]
    return (scaled[:, :, None].astype(jnp.bfloat16), channel_power)


def step(alm, beam, m_table, chan_mask, noise):
    sizes = [lax.axis_size(name) for name in ("ma", "freq", "pol")]
    if alm.shape[2] % 128 == 0 and sizes == [4, 2, 2]:
        return on_device(alm, beam, m_table, chan_mask, noise)
    return on_device_plain(alm, beam, m_table, chan_mask, noise)


def solution(mesh):
    return jax.shard_map(
        step,
        mesh=mesh,
        in_specs=(
            P(None, "freq", ("ma", "pol"), None, "sky"),
            P("ma", "freq", None, "pol", None),
            P("ma"),
            P("freq"),
            P("freq", "pol"),
        ),
        out_specs=(P(None, "freq", "ma", "pol", "sky"), P(("sky", "freq"))),
        check_vma=False,
    )
```

```python
import functools

import jax
import jax.numpy as jnp
from jax import lax
from jax.experimental import pallas as pl
from jax.experimental.pallas import tpu as pltpu
from jax.sharding import PartitionSpec as P

VMEM = pl.BlockSpec(memory_space=pltpu.VMEM)
SMEM = pl.BlockSpec(memory_space=pltpu.SMEM)
HBM = pl.BlockSpec(memory_space=pltpu.HBM)


def column(row):
    return jnp.transpose(jnp.broadcast_to(row, (128, row.shape[1])))


def split_kernel(steps, alm_ref, *refs):
    *slab_refs, modes_ref = refs
    place = lax.axis_index("ma")
    for c in range(alm_ref.shape[0]):
        modes_ref[...] = pltpu.einshape("lms->mls", alm_ref[c])
        for ref, step in zip(slab_refs, steps, strict=True):
            ref[c] = modes_ref[place ^ step]


def load_kernel(beam_ref, noise_ref, left_ref, weight_ref, sems):
    _, _, total = beam_ref.shape
    blocks = left_ref.shape[0]
    ell = total // blocks
    copies = []
    for block in range(blocks):
        for c in range(2):
            copies.append(
                pltpu.make_async_copy(
                    beam_ref.at[c, :, pl.ds(block * ell, ell)],
                    left_ref.at[block, :, pl.ds(c * ell, ell)],
                    sems.at[2 * block + c],
                )
            )
            copies[-1].start()
    weight_ref[...] = column(lax.rsqrt(noise_ref[...]))
    for copy in copies:
        copy.wait()


def contract(m_ref, left_ref, block_refs, steps):
    ell = block_refs[0].shape[1]
    left, right_real, right_imag = [], [], []
    for ref, (step, other) in zip(block_refs, steps, strict=True):
        owner = lax.axis_index("ma") ^ step
        half = lax.axis_index("pol") ^ other
        block = owner * lax.axis_size("pol") + half
        degree = block * ell + lax.broadcasted_iota(jnp.int32, (ell, ref.shape[2]), 0)
        keep = degree >= m_ref[0]
        real = jnp.where(keep, ref[0], jnp.zeros((), ref.dtype))
        imag = jnp.where(keep, ref[1], jnp.zeros((), ref.dtype))
        left.append(left_ref[block])
        right_real += [real, -imag]
        right_imag += [imag, real]
    left = jnp.concatenate(left, axis=1)
    dot = functools.partial(jnp.dot, preferred_element_type=jnp.float32)
    return (
        dot(left, jnp.concatenate(right_real, axis=0)),
        dot(left, jnp.concatenate(right_imag, axis=0)),
    )


def first_kernel(steps, m_ref, mask_ref, left_ref, *refs):
    del mask_ref
    *blocks, vis_ref = refs
    vis_ref[0], vis_ref[1] = contract(m_ref, left_ref, blocks, steps)


def weigh(vis, weight):
    return jnp.concatenate(
        [vis[:, i : i + 128] * weight for i in range(0, vis.shape[1], 128)], axis=1
    )


def power_of(real, imag):
    squares = real * real + imag * imag
    folded = functools.reduce(
        jnp.add, [squares[:, i : i + 128] for i in range(0, squares.shape[1], 128)]
    )
    return jnp.sum(folded)


def next_kernel(steps, m_ref, left_ref, before_ref, *refs):
    *blocks, vis_ref = refs
    real, imag = contract(m_ref, left_ref, blocks, steps)
    vis_ref[0] = real + before_ref[0]
    vis_ref[1] = imag + before_ref[1]


def last_kernel(steps, slots, m_ref, mask_ref, left_ref, weight_ref, before_ref, *refs):
    *blocks, vis_ref, power_ref = refs
    real, imag = contract(m_ref, left_ref, blocks, steps)
    weight = weight_ref[...]
    real = weigh(real + before_ref[0], weight)
    imag = weigh(imag + before_ref[1], weight)
    vis_ref[0] = real
    vis_ref[1] = imag
    total = power_of(real, imag)
    lane = lax.broadcasted_iota(jnp.int32, power_ref.shape, 1)
    leader = (lax.axis_index("ma") == 0) & (lax.axis_index("pol") == 0)
    live = jnp.where(leader, mask_ref[0], 0).astype(jnp.float32)
    channel = lax.axis_index("freq")
    power_ref[...] = jnp.where(lane == channel, total, 0.0) + jnp.where(
        lane == channel + slots, live, 0.0
    )


def finish_kernel(slots, modes, mask_ref, total_ref, vis_ref, scaled_ref, power_ref, held_ref, own_ref, sems):
    lane = lax.broadcasted_iota(jnp.int32, (1, 128), 1)
    totals = total_ref[0:1, :]
    powers = totals / modes
    masks = pltpu.roll(totals, 128 - slots, 1)

    def over(where, values):
        return jnp.sum(jnp.where(where, values, 0.0), axis=1, keepdims=True)

    band = over(lane < slots, powers * masks) / over(lane < slots, masks)
    own = over(lane == lax.axis_index("freq"), powers)
    mask = mask_ref[0].astype(jnp.float32)
    factor = mask / jnp.sqrt(0.5 * own + 0.5 * band + 1e-06)
    own_ref[...] = jnp.where(lane == 0, own, 0.0)
    copies = [pltpu.make_async_copy(own_ref, power_ref, sems.at[0])]
    copies[0].start()
    parts, rows, _ = vis_ref.shape
    chunk = rows // 4
    for c in range(parts):
        for j in range(0, rows, chunk):
            held_ref[c, j : j + chunk] = (vis_ref[c, j : j + chunk] * factor).astype(
                scaled_ref.dtype
            )
            copies.append(
                pltpu.make_async_copy(
                    held_ref.at[c, pl.ds(j, chunk)],
                    scaled_ref.at[c, pl.ds(j, chunk)],
                    sems.at[len(copies)],
                )
            )
            copies[-1].start()
    for copy in copies:
        copy.wait()


def straight(x, name, step):
    size = lax.axis_size(name)
    return lax.ppermute(x, name, [(i, i ^ step) for i in range(size)])


def swap(x, name, step):
    names, flip = ("pol", step) if name == "pol" else ((name, "pol"), 2 * step + 1)
    size = lax.axis_size(names)
    return lax.ppermute(x, names, [(i, i ^ flip) for i in range(size)])


def on_device(alm, beam, m_table, chan_mask, noise):
    n_ma, n_pol, n_freq = (lax.axis_size(name) for name in ("ma", "pol", "freq"))
    parts, _, ell, _, maps = alm.shape
    modes = beam.shape[3]
    response = beam[0, 0]
    params = pltpu.CompilerParams(vmem_limit_bytes=24 << 20)
    vis_shape = jax.ShapeDtypeStruct((parts, modes, maps), jnp.float32)
    slab = jax.ShapeDtypeStruct((parts, ell, maps), alm.dtype)
    row = jax.ShapeDtypeStruct((8, 128), jnp.float32)
    weights = jax.ShapeDtypeStruct((modes, 128), jnp.float32)

    def call(kernel, out_shape, scalars, operands, blocks, **more):
        return pl.pallas_call(
            kernel,
            out_shape=out_shape,
            in_specs=more.pop("in_specs", [SMEM] * len(scalars) + [VMEM] * len(operands)),
            out_specs=more.pop("out_specs", jax.tree.map(lambda _: VMEM, out_shape)),
            compiler_params=params,
            cost_estimate=pl.CostEstimate(
                flops=blocks * 2 * 4 * modes * maps * ell,
                bytes_accessed=(blocks + 4) * parts * ell * (maps + modes) * 2,
                transcendentals=0,
            ),
            **more,
        )(*scalars, *operands)

    three, one, two, own = call(
        functools.partial(split_kernel, (3, 1, 2, 0)),
        [slab] * n_ma,
        (),
        (alm[:, 0],),
        0,
        scratch_shapes=[pltpu.VMEM((n_ma, ell, maps), alm.dtype)],
    )
    three = straight(three, "ma", 3)
    one = straight(one, "ma", 1)
    two = straight(two, "ma", 2)
    own_far = swap(own, "pol", 1)
    one_far = swap(one, "pol", 1)
    three_far = swap(three, "pol", 1)
    two_far = swap(two, "pol", 1)
    blocks = n_ma * n_pol
    left, weight = call(
        load_kernel,
        (jax.ShapeDtypeStruct((blocks, modes, 2 * ell), beam.dtype), weights),
        (),
        (response, noise),
        0,
        in_specs=[HBM, VMEM],
        scratch_shapes=[pltpu.SemaphoreType.DMA((2 * blocks,))],
    )
    steps = ((0, 0), (0, 1), (1, 0), (1, 1), (2, 0), (2, 1))
    vis = call(
        functools.partial(first_kernel, steps),
        vis_shape,
        (m_table, chan_mask),
        (left, own, own_far, one, one_far, two, two_far),
        6,
    )
    vis = call(
        functools.partial(next_kernel, ((3, 0),)), vis_shape, (m_table,), (left, vis, three), 1
    )
    vis, total = call(
        functools.partial(last_kernel, ((3, 1),), n_freq),
        (vis_shape, row),
        (m_table, chan_mask),
        (left, weight, vis, three_far),
        1,
    )
    for name, step in (('pol', 1), ('freq', 1), ('ma', 3), ('ma', 1)):
        total = total + swap(total, name, step)
    scaled, own_power = call(
        functools.partial(finish_kernel, n_freq, n_ma * n_pol * modes * maps),
        (
            jax.ShapeDtypeStruct((parts, modes, maps), jnp.bfloat16),
            jax.ShapeDtypeStruct((1, 128), jnp.float32),
        ),
        (chan_mask,),
        (total, vis),
        0,
        out_specs=(HBM, HBM),
        scratch_shapes=[
            pltpu.VMEM((parts, modes, maps), jnp.bfloat16),
            pltpu.VMEM((1, 128), jnp.float32),
            pltpu.SemaphoreType.DMA((4 * parts + 1,)),
        ],
    )
    return scaled[:, None, None], own_power[0, :1]


def on_device_plain(alm, beam, m_table, chan_mask, noise):
    arrived = lax.all_to_all(alm, "ma", split_axis=3, concat_axis=2, tiled=True)
    blocks = arrived.reshape(
        arrived.shape[0],
        arrived.shape[1],
        lax.axis_size("ma"),
        arrived.shape[2] // lax.axis_size("ma"),
        arrived.shape[4],
    )
    joined = lax.all_gather(blocks, "pol", axis=3, tiled=True)
    coeffs_all = joined.reshape(
        joined.shape[0], joined.shape[1], joined.shape[2] * joined.shape[3], joined.shape[4]
    )
    degree = lax.iota(jnp.int32, coeffs_all.shape[2])
    keep_mask = (degree >= m_table[0])[None, None, :, None]
    coeffs = jnp.where(keep_mask, coeffs_all, jnp.zeros((), coeffs_all.dtype))
    response = beam[0]
    real_part = jnp.einsum(
        "fkl,fls->fks", response[:, 0], coeffs[0], preferred_element_type=jnp.float32
    ) - jnp.einsum("fkl,fls->fks", response[:, 1], coeffs[1], preferred_element_type=jnp.float32)
    imag_part = jnp.einsum(
        "fkl,fls->fks", response[:, 0], coeffs[1], preferred_element_type=jnp.float32
    ) + jnp.einsum("fkl,fls->fks", response[:, 1], coeffs[0], preferred_element_type=jnp.float32)
    visibility = jnp.stack([real_part, imag_part])
    weighted = visibility * visibility / noise[None, :, :, None]
    partial_power = jnp.sum(weighted, axis=(0, 2, 3))
    modes_total = jnp.float32(
        lax.axis_size("ma") * noise.shape[1] * lax.axis_size("pol") * visibility.shape[3]
    )
    mask_float = chan_mask.astype(jnp.float32)
    channel_power = lax.psum(partial_power, ("ma", "pol")) / modes_total
    masked_sum, live_count = lax.psum(
        (jnp.sum(mask_float * channel_power), jnp.sum(mask_float)), "freq"
    )
    band_power = masked_sum / live_count
    factor = mask_float / jnp.sqrt(0.5 * channel_power + 0.5 * band_power + 1e-06)
    scaled = visibility * (lax.rsqrt(noise) * factor[:, None])[None, :, :, None]
    return (scaled[:, :, None].astype(jnp.bfloat16), channel_power)


def step(alm, beam, m_table, chan_mask, noise):
    sizes = [lax.axis_size(name) for name in ("ma", "freq", "pol")]
    if alm.shape[2] % 128 == 0 and sizes == [4, 2, 2]:
        return on_device(alm, beam, m_table, chan_mask, noise)
    return on_device_plain(alm, beam, m_table, chan_mask, noise)


def solution(mesh):
    return jax.shard_map(
        step,
        mesh=mesh,
        in_specs=(
            P(None, "freq", ("ma", "pol"), None, "sky"),
            P("ma", "freq", None, "pol", None),
            P("ma"),
            P("freq"),
            P("freq", "pol"),
        ),
        out_specs=(P(None, "freq", "ma", "pol", "sky"), P(("sky", "freq"))),
        check_vma=False,
    )
```

```python
import functools

import jax
import jax.numpy as jnp
from jax import lax
from jax.experimental import pallas as pl
from jax.experimental.pallas import tpu as pltpu
from jax.sharding import PartitionSpec as P

VMEM = pl.BlockSpec(memory_space=pltpu.VMEM)
SMEM = pl.BlockSpec(memory_space=pltpu.SMEM)
HBM = pl.BlockSpec(memory_space=pltpu.HBM)


def column(row):
    return jnp.transpose(jnp.broadcast_to(row, (128, row.shape[1])))


def maps_of(pol, count):
    return pl.ds(pl.multiple_of(pol * count, count), count)


def split_kernel(pieces, alm_ref, *refs):
    *slab_refs, held_ref, modes_ref, sems = refs
    place, pol = lax.axis_index("ma"), lax.axis_index("pol")
    parts, ell = alm_ref.shape[:2]
    chunks = 2
    size = ell // chunks
    copies = {}
    for c in range(parts):
        for j in range(chunks):
            rows = pl.ds(j * size, size)
            copies[c, j] = pltpu.make_async_copy(
                alm_ref.at[c, rows], held_ref.at[c, rows], sems.at[c * chunks + j]
            )
            copies[c, j].start()
    for (c, j), copy in copies.items():
        copy.wait()
        rows = slice(j * size, (j + 1) * size)
        modes_ref[...] = pltpu.einshape("lms->mls", held_ref[c, rows])
        for ref, (step, other) in zip(slab_refs, pieces, strict=True):
            if other is None:
                ref[c, rows] = modes_ref[place ^ step]
            else:
                ref[c, rows] = modes_ref[place ^ step, :, maps_of(pol ^ other, ref.shape[2])]


def load_kernel(step, beam_ref, noise_ref, left_ref, share_ref, weight_ref, sems):
    blocks = left_ref.shape[0]
    ell = beam_ref.shape[2] // blocks
    copies = []
    for block in range(blocks):
        for c in range(2):
            copies.append(
                pltpu.make_async_copy(
                    beam_ref.at[c, :, pl.ds(block * ell, ell)],
                    left_ref.at[block, :, pl.ds(c * ell, ell)],
                    sems.at[2 * block + c],
                )
            )
            copies[-1].start()
    weight_ref[...] = column(lax.rsqrt(noise_ref[...]))
    for copy in copies:
        copy.wait()
    for half in range(share_ref.shape[0]):
        share_ref[half] = left_ref[(lax.axis_index("ma") ^ step) * lax.axis_size("pol") + half]


def operands(m_ref, block_refs, steps, maps):
    ell = block_refs[0].shape[1]
    blocks, right_real, right_imag = [], [], []
    for ref, (step, other) in zip(block_refs, steps, strict=True):
        owner = lax.axis_index("ma") ^ step
        half = lax.axis_index("pol") ^ other
        block = owner * lax.axis_size("pol") + half
        real, imag = ref[0, :, maps], ref[1, :, maps]
        degree = block * ell + lax.broadcasted_iota(jnp.int32, real.shape, 0)
        keep = degree >= m_ref[0]
        real = jnp.where(keep, real, jnp.zeros((), ref.dtype))
        imag = jnp.where(keep, imag, jnp.zeros((), ref.dtype))
        blocks.append(block)
        right_real += [real, -imag]
        right_imag += [imag, real]
    return blocks, jnp.concatenate(right_real, axis=0), jnp.concatenate(right_imag, axis=0)


dot = functools.partial(jnp.dot, preferred_element_type=jnp.float32)


def first_kernel(steps, m_ref, mask_ref, left_ref, *refs):
    del mask_ref
    *block_refs, mine_ref, give_ref = refs
    pol, count = lax.axis_index("pol"), mine_ref.shape[2]
    for ref, owner in ((mine_ref, pol), (give_ref, pol ^ 1)):
        blocks, *rights = operands(m_ref, block_refs, steps, maps_of(owner, count))
        left = jnp.concatenate([left_ref[block] for block in blocks], axis=1)
        for c, right in enumerate(rights):
            ref[c] = dot(left, right)


def same_kernel(step, m_ref, left_ref, share_ref, mine_ref, got_ref, block_ref, near_ref, far_ref):
    (block,), *rights = operands(m_ref, [block_ref], [(step, 0)], slice(None))
    shared = share_ref[lax.axis_index("pol")]
    for c, right in enumerate(rights):
        near_ref[c] = mine_ref[c] + dot(left_ref[block], right)
        far_ref[c] = got_ref[c] + dot(shared, right)


def weigh(vis, weight):
    return jnp.concatenate(
        [vis[:, i : i + 128] * weight for i in range(0, vis.shape[1], 128)], axis=1
    )


def last_kernel(
    step,
    slots,
    m_ref,
    mask_ref,
    left_ref,
    share_ref,
    weight_ref,
    other_ref,
    mine_ref,
    got_ref,
    block_ref,
    near_ref,
    far_ref,
    power_ref,
):
    (block,), *rights = operands(m_ref, [block_ref], [(step, 1)], slice(None))
    sums = jnp.zeros(weight_ref.shape, jnp.float32)
    for left, before_ref, weights_ref, ref in (
        (share_ref[lax.axis_index("pol") ^ 1], got_ref, other_ref, far_ref),
        (left_ref[block], mine_ref, weight_ref, near_ref),
    ):
        weight = weights_ref[...]
        for c, right in enumerate(rights):
            vis = weigh(before_ref[c] + dot(left, right), weight)
            ref[c] = vis
            for i in range(0, vis.shape[1], 128):
                sums += vis[:, i : i + 128] * vis[:, i : i + 128]
    total = jnp.sum(sums)
    lane = lax.broadcasted_iota(jnp.int32, power_ref.shape, 1)
    leader = (lax.axis_index("ma") == 0) & (lax.axis_index("pol") == 0)
    live = jnp.where(leader, mask_ref[0], 0).astype(jnp.float32)
    channel = lax.axis_index("freq")
    power_ref[...] = jnp.where(lane == channel, total, 0.0) + jnp.where(
        lane == channel + slots, live, 0.0
    )


def finish_kernel(slots, modes, mask_ref, total_ref, near_ref, got_ref, scaled_ref, power_ref, held_ref, own_ref, sems):
    lane = lax.broadcasted_iota(jnp.int32, (1, 128), 1)
    totals = total_ref[0:1, :]
    powers = totals / modes
    masks = pltpu.roll(totals, 128 - slots, 1)

    def over(where, values):
        return jnp.sum(jnp.where(where, values, 0.0), axis=1, keepdims=True)

    band = over(lane < slots, powers * masks) / over(lane < slots, masks)
    own = over(lane == lax.axis_index("freq"), powers)
    mask = mask_ref[0].astype(jnp.float32)
    factor = mask / jnp.sqrt(0.5 * own + 0.5 * band + 1e-06)
    own_ref[...] = jnp.where(lane == 0, own, 0.0)
    copies = [pltpu.make_async_copy(own_ref, power_ref, sems.at[0])]
    copies[0].start()
    parts, rows, count = near_ref.shape
    pol = lax.axis_index("pol")
    chunk = rows // 2
    for c in range(parts):
        for j in range(0, rows, chunk):
            for half, (ref, owner) in enumerate(((near_ref, pol), (got_ref, pol ^ 1))):
                held_ref[half, c, j : j + chunk] = (ref[c, j : j + chunk] * factor).astype(
                    scaled_ref.dtype
                )
                copies.append(
                    pltpu.make_async_copy(
                        held_ref.at[half, c, pl.ds(j, chunk)],
                        scaled_ref.at[c, pl.ds(j, chunk), maps_of(owner, count)],
                        sems.at[len(copies)],
                    )
                )
                copies[-1].start()
    for copy in copies:
        copy.wait()


def straight(x, name, step):
    size = lax.axis_size(name)
    return lax.ppermute(x, name, [(i, i ^ step) for i in range(size)])


def swap(x, name, step):
    names, flip = ("pol", step) if name == "pol" else ((name, "pol"), 2 * step + 1)
    size = lax.axis_size(names)
    return lax.ppermute(x, names, [(i, i ^ flip) for i in range(size)])


def on_device(alm, beam, m_table, chan_mask, noise):
    n_ma, n_pol, n_freq = (lax.axis_size(name) for name in ("ma", "pol", "freq"))
    parts, _, ell, _, maps = alm.shape
    modes = beam.shape[3]
    response = beam[0, 0]
    params = pltpu.CompilerParams(vmem_limit_bytes=24 << 20)

    def visible(count):
        return jax.ShapeDtypeStruct((parts, modes, count), jnp.float32)

    def slab(count):
        return jax.ShapeDtypeStruct((parts, ell, count), alm.dtype)

    row = jax.ShapeDtypeStruct((8, 128), jnp.float32)
    weights = jax.ShapeDtypeStruct((modes, 128), jnp.float32)

    def call(kernel, out_shape, scalars, operands, blocks, **more):
        return pl.pallas_call(
            kernel,
            out_shape=out_shape,
            in_specs=more.pop("in_specs", [SMEM] * len(scalars) + [VMEM] * len(operands)),
            out_specs=more.pop("out_specs", jax.tree.map(lambda _: VMEM, out_shape)),
            compiler_params=more.pop("compiler_params", params),
            cost_estimate=pl.CostEstimate(
                flops=blocks * 2 * 4 * modes * maps * ell,
                bytes_accessed=(blocks + 4) * parts * ell * (maps + modes) * 2,
                transcendentals=0,
            ),
            **more,
        )(*scalars, *operands)

    half = maps // n_pol
    pieces = ((2, None), (1, None), (3, 0), (3, 1), (0, None))
    two, one, same, cross, own = call(
        functools.partial(split_kernel, pieces),
        [slab(maps if other is None else half) for _, other in pieces],
        (),
        (pltpu.with_memory_space_constraint(alm[:, 0], pltpu.HBM),),
        0,
        in_specs=[HBM],
        scratch_shapes=[
            pltpu.VMEM((parts, ell, n_ma, maps), alm.dtype),
            pltpu.VMEM((n_ma, ell // 2, maps), alm.dtype),
            pltpu.SemaphoreType.DMA((2 * parts,)),
        ],
    )
    two = straight(two, "ma", 2)
    one = straight(one, "ma", 1)
    same = straight(same, "ma", 3)
    cross = swap(cross, "ma", 3)
    own_far = swap(own, "pol", 1)
    one_far = swap(one, "pol", 1)
    two_far = swap(two, "pol", 1)
    blocks = n_ma * n_pol
    left, share, weight = call(
        functools.partial(load_kernel, 3),
        (
            jax.ShapeDtypeStruct((blocks, modes, 2 * ell), beam.dtype),
            jax.ShapeDtypeStruct((n_pol, modes, 2 * ell), beam.dtype),
            weights,
        ),
        (),
        (pltpu.with_memory_space_constraint(response, pltpu.HBM), noise),
        0,
        in_specs=[HBM, VMEM],
        scratch_shapes=[pltpu.SemaphoreType.DMA((2 * blocks,))],
    )
    share = swap(share, "pol", 1)
    other_weight = swap(weight, "pol", 1)
    steps = ((0, 0), (0, 1), (1, 0), (1, 1), (2, 0), (2, 1))
    mine, give = call(
        functools.partial(first_kernel, steps),
        (visible(half), visible(half)),
        (m_table, chan_mask),
        (left, own, own_far, one, one_far, two, two_far),
        6,
    )
    got = swap(give, "pol", 1)
    mine, got = call(
        functools.partial(same_kernel, 3),
        (visible(half), visible(half)),
        (m_table,),
        (left, share, mine, got, same),
        1,
    )
    near, far, total = call(
        functools.partial(last_kernel, 3, n_freq),
        (visible(half), visible(half), row),
        (m_table, chan_mask),
        (left, share, weight, other_weight, mine, got, cross),
        1,
    )
    far = swap(far, "pol", 1)
    for name, step in (("pol", 1), ("freq", 1), ("ma", 3), ("ma", 1)):
        total = total + swap(total, name, step)
    scaled, own_power = call(
        functools.partial(finish_kernel, n_freq, n_ma * n_pol * modes * maps),
        (
            jax.ShapeDtypeStruct((parts, modes, maps), jnp.bfloat16),
            jax.ShapeDtypeStruct((1, 128), jnp.float32),
        ),
        (chan_mask,),
        (total, near, far),
        0,
        out_specs=(HBM, HBM),
        scratch_shapes=[
            pltpu.VMEM((n_pol, parts, modes, half), jnp.bfloat16),
            pltpu.VMEM((1, 128), jnp.float32),
            pltpu.SemaphoreType.DMA((4 * parts + 1,)),
        ],
    )
    return scaled[:, None, None], own_power[0, :1]


def on_device_plain(alm, beam, m_table, chan_mask, noise):
    arrived = lax.all_to_all(alm, "ma", split_axis=3, concat_axis=2, tiled=True)
    blocks = arrived.reshape(
        arrived.shape[0],
        arrived.shape[1],
        lax.axis_size("ma"),
        arrived.shape[2] // lax.axis_size("ma"),
        arrived.shape[4],
    )
    joined = lax.all_gather(blocks, "pol", axis=3, tiled=True)
    coeffs_all = joined.reshape(
        joined.shape[0], joined.shape[1], joined.shape[2] * joined.shape[3], joined.shape[4]
    )
    degree = lax.iota(jnp.int32, coeffs_all.shape[2])
    keep_mask = (degree >= m_table[0])[None, None, :, None]
    coeffs = jnp.where(keep_mask, coeffs_all, jnp.zeros((), coeffs_all.dtype))
    response = beam[0]
    real_part = jnp.einsum(
        "fkl,fls->fks", response[:, 0], coeffs[0], preferred_element_type=jnp.float32
    ) - jnp.einsum("fkl,fls->fks", response[:, 1], coeffs[1], preferred_element_type=jnp.float32)
    imag_part = jnp.einsum(
        "fkl,fls->fks", response[:, 0], coeffs[1], preferred_element_type=jnp.float32
    ) + jnp.einsum("fkl,fls->fks", response[:, 1], coeffs[0], preferred_element_type=jnp.float32)
    visibility = jnp.stack([real_part, imag_part])
    weighted = visibility * visibility / noise[None, :, :, None]
    partial_power = jnp.sum(weighted, axis=(0, 2, 3))
    modes_total = jnp.float32(
        lax.axis_size("ma") * noise.shape[1] * lax.axis_size("pol") * visibility.shape[3]
    )
    mask_float = chan_mask.astype(jnp.float32)
    channel_power = lax.psum(partial_power, ("ma", "pol")) / modes_total
    masked_sum, live_count = lax.psum(
        (jnp.sum(mask_float * channel_power), jnp.sum(mask_float)), "freq"
    )
    band_power = masked_sum / live_count
    factor = mask_float / jnp.sqrt(0.5 * channel_power + 0.5 * band_power + 1e-06)
    scaled = visibility * (lax.rsqrt(noise) * factor[:, None])[None, :, :, None]
    return (scaled[:, :, None].astype(jnp.bfloat16), channel_power)


def step(alm, beam, m_table, chan_mask, noise):
    sizes = [lax.axis_size(name) for name in ("ma", "freq", "pol")]
    if alm.shape[2] % 128 == 0 and sizes == [4, 2, 2]:
        return on_device(alm, beam, m_table, chan_mask, noise)
    return on_device_plain(alm, beam, m_table, chan_mask, noise)


def solution(mesh):
    return jax.shard_map(
        step,
        mesh=mesh,
        in_specs=(
            P(None, "freq", ("ma", "pol"), None, "sky"),
            P("ma", "freq", None, "pol", None),
            P("ma"),
            P("freq"),
            P("freq", "pol"),
        ),
        out_specs=(P(None, "freq", "ma", "pol", "sky"), P(("sky", "freq"))),
        check_vma=False,
    )
```

```python
import functools

import jax
import jax.numpy as jnp
from jax import lax
from jax.experimental import pallas as pl
from jax.experimental.pallas import tpu as pltpu
from jax.sharding import PartitionSpec as P

VMEM = pl.BlockSpec(memory_space=pltpu.VMEM)
SMEM = pl.BlockSpec(memory_space=pltpu.SMEM)
HBM = pl.BlockSpec(memory_space=pltpu.HBM)


def column(row):
    return jnp.transpose(jnp.broadcast_to(row, (128, row.shape[1])))


def maps_of(pol, count):
    return pl.ds(pl.multiple_of(pol * count, count), count)


def split_kernel(pieces, alm_ref, *refs):
    *slab_refs, held_ref, modes_ref, sems = refs
    place, pol = lax.axis_index("ma"), lax.axis_index("pol")
    parts, ell = alm_ref.shape[:2]
    chunks = 2
    size = ell // chunks
    copies = {}
    for c in range(parts):
        for j in range(chunks):
            rows = pl.ds(j * size, size)
            copies[c, j] = pltpu.make_async_copy(
                alm_ref.at[c, rows], held_ref.at[c, rows], sems.at[c * chunks + j]
            )
            copies[c, j].start()
    for (c, j), copy in copies.items():
        copy.wait()
        rows = slice(j * size, (j + 1) * size)
        modes_ref[...] = pltpu.einshape("lms->mls", held_ref[c, rows])
        for ref, (step, other) in zip(slab_refs, pieces, strict=True):
            if other is None:
                ref[c, rows] = modes_ref[place ^ step]
            else:
                ref[c, rows] = modes_ref[place ^ step, :, maps_of(pol ^ other, ref.shape[2])]


def load_kernel(step, beam_ref, noise_ref, left_ref, share_ref, weight_ref, sems):
    blocks = left_ref.shape[0]
    ell = beam_ref.shape[2] // blocks
    copies = []
    for block in range(blocks):
        for c in range(2):
            copies.append(
                pltpu.make_async_copy(
                    beam_ref.at[c, :, pl.ds(block * ell, ell)],
                    left_ref.at[block, :, pl.ds(c * ell, ell)],
                    sems.at[2 * block + c],
                )
            )
            copies[-1].start()
    weight_ref[...] = column(lax.rsqrt(noise_ref[...]))
    for copy in copies:
        copy.wait()
    for half in range(share_ref.shape[0]):
        share_ref[half] = left_ref[(lax.axis_index("ma") ^ step) * lax.axis_size("pol") + half]


def operands(m_ref, block_refs, steps, maps):
    ell = block_refs[0].shape[1]
    blocks, right_real, right_imag = [], [], []
    for ref, (step, other) in zip(block_refs, steps, strict=True):
        owner = lax.axis_index("ma") ^ step
        half = lax.axis_index("pol") ^ other
        block = owner * lax.axis_size("pol") + half
        real, imag = ref[0, :, maps], ref[1, :, maps]
        degree = block * ell + lax.broadcasted_iota(jnp.int32, real.shape, 0)
        keep = degree >= m_ref[0]
        real = jnp.where(keep, real, jnp.zeros((), ref.dtype))
        imag = jnp.where(keep, imag, jnp.zeros((), ref.dtype))
        blocks.append(block)
        right_real += [real, -imag]
        right_imag += [imag, real]
    return blocks, jnp.concatenate(right_real, axis=0), jnp.concatenate(right_imag, axis=0)


dot = functools.partial(jnp.dot, preferred_element_type=jnp.float32)


def first_kernel(steps, other, m_ref, mask_ref, left_ref, *refs):
    del mask_ref
    *block_refs, vis_ref = refs
    maps = maps_of(lax.axis_index("pol") ^ other, vis_ref.shape[2])
    blocks, *rights = operands(m_ref, block_refs, steps, maps)
    left = jnp.concatenate([left_ref[block] for block in blocks], axis=1)
    for c, right in enumerate(rights):
        vis_ref[c] = dot(left, right)


def same_kernel(step, m_ref, left_ref, share_ref, mine_ref, got_ref, block_ref, near_ref, far_ref):
    (block,), *rights = operands(m_ref, [block_ref], [(step, 0)], slice(None))
    shared = share_ref[lax.axis_index("pol")]
    for c, right in enumerate(rights):
        near_ref[c] = mine_ref[c] + dot(left_ref[block], right)
        far_ref[c] = got_ref[c] + dot(shared, right)


def weigh(vis, weight):
    return jnp.concatenate(
        [vis[:, i : i + 128] * weight for i in range(0, vis.shape[1], 128)], axis=1
    )


def last_kernel(
    step,
    slots,
    m_ref,
    mask_ref,
    left_ref,
    share_ref,
    weight_ref,
    other_ref,
    mine_ref,
    got_ref,
    block_ref,
    near_ref,
    far_ref,
    power_ref,
):
    (block,), *rights = operands(m_ref, [block_ref], [(step, 1)], slice(None))
    sums = jnp.zeros(weight_ref.shape, jnp.float32)
    for left, before_ref, weights_ref, ref in (
        (share_ref[lax.axis_index("pol") ^ 1], got_ref, other_ref, far_ref),
        (left_ref[block], mine_ref, weight_ref, near_ref),
    ):
        weight = weights_ref[...]
        for c, right in enumerate(rights):
            vis = weigh(before_ref[c] + dot(left, right), weight)
            ref[c] = vis
            for i in range(0, vis.shape[1], 128):
                sums += vis[:, i : i + 128] * vis[:, i : i + 128]
    total = jnp.sum(sums)
    lane = lax.broadcasted_iota(jnp.int32, power_ref.shape, 1)
    leader = (lax.axis_index("ma") == 0) & (lax.axis_index("pol") == 0)
    live = jnp.where(leader, mask_ref[0], 0).astype(jnp.float32)
    channel = lax.axis_index("freq")
    power_ref[...] = jnp.where(lane == channel, total, 0.0) + jnp.where(
        lane == channel + slots, live, 0.0
    )


def finish_kernel(slots, modes, mask_ref, total_ref, near_ref, got_ref, scaled_ref, power_ref, held_ref, own_ref, sems):
    lane = lax.broadcasted_iota(jnp.int32, (1, 128), 1)
    totals = total_ref[0:1, :]
    powers = totals / modes
    masks = pltpu.roll(totals, 128 - slots, 1)

    def over(where, values):
        return jnp.sum(jnp.where(where, values, 0.0), axis=1, keepdims=True)

    band = over(lane < slots, powers * masks) / over(lane < slots, masks)
    own = over(lane == lax.axis_index("freq"), powers)
    mask = mask_ref[0].astype(jnp.float32)
    factor = mask / jnp.sqrt(0.5 * own + 0.5 * band + 1e-06)
    own_ref[...] = jnp.where(lane == 0, own, 0.0)
    copies = [pltpu.make_async_copy(own_ref, power_ref, sems.at[0])]
    copies[0].start()
    parts, rows, count = near_ref.shape
    pol = lax.axis_index("pol")
    chunk = rows // 2
    for c in range(parts):
        for j in range(0, rows, chunk):
            for half, (ref, owner) in enumerate(((near_ref, pol), (got_ref, pol ^ 1))):
                held_ref[half, c, j : j + chunk] = (ref[c, j : j + chunk] * factor).astype(
                    scaled_ref.dtype
                )
                copies.append(
                    pltpu.make_async_copy(
                        held_ref.at[half, c, pl.ds(j, chunk)],
                        scaled_ref.at[c, pl.ds(j, chunk), maps_of(owner, count)],
                        sems.at[len(copies)],
                    )
                )
                copies[-1].start()
    for copy in copies:
        copy.wait()


def straight(x, name, step):
    size = lax.axis_size(name)
    return lax.ppermute(x, name, [(i, i ^ step) for i in range(size)])


def swap(x, name, step):
    names, flip = ("pol", step) if name == "pol" else ((name, "pol"), 2 * step + 1)
    size = lax.axis_size(names)
    return lax.ppermute(x, names, [(i, i ^ flip) for i in range(size)])


def on_device(alm, beam, m_table, chan_mask, noise):
    n_ma, n_pol, n_freq = (lax.axis_size(name) for name in ("ma", "pol", "freq"))
    parts, _, ell, _, maps = alm.shape
    modes = beam.shape[3]
    response = beam[0, 0]
    params = pltpu.CompilerParams(vmem_limit_bytes=24 << 20)

    def visible(count):
        return jax.ShapeDtypeStruct((parts, modes, count), jnp.float32)

    def slab(count):
        return jax.ShapeDtypeStruct((parts, ell, count), alm.dtype)

    row = jax.ShapeDtypeStruct((8, 128), jnp.float32)
    weights = jax.ShapeDtypeStruct((modes, 128), jnp.float32)

    def call(kernel, out_shape, scalars, operands, blocks, **more):
        return pl.pallas_call(
            kernel,
            out_shape=out_shape,
            in_specs=more.pop("in_specs", [SMEM] * len(scalars) + [VMEM] * len(operands)),
            out_specs=more.pop("out_specs", jax.tree.map(lambda _: VMEM, out_shape)),
            compiler_params=more.pop("compiler_params", params),
            cost_estimate=pl.CostEstimate(
                flops=blocks * 2 * 4 * modes * maps * ell,
                bytes_accessed=(blocks + 4) * parts * ell * (maps + modes) * 2,
                transcendentals=0,
            ),
            **more,
        )(*scalars, *operands)

    half = maps // n_pol
    pieces = ((2, None), (1, None), (3, 0), (3, 1), (0, None))
    two, one, same, cross, own = call(
        functools.partial(split_kernel, pieces),
        [slab(maps if other is None else half) for _, other in pieces],
        (),
        (pltpu.with_memory_space_constraint(alm[:, 0], pltpu.HBM),),
        0,
        in_specs=[HBM],
        scratch_shapes=[
            pltpu.VMEM((parts, ell, n_ma, maps), alm.dtype),
            pltpu.VMEM((n_ma, ell // 2, maps), alm.dtype),
            pltpu.SemaphoreType.DMA((2 * parts,)),
        ],
    )
    two = straight(two, "ma", 2)
    one = straight(one, "ma", 1)
    same = straight(same, "ma", 3)
    cross = swap(cross, "ma", 3)
    own_far = swap(own, "pol", 1)
    one_far = swap(one, "pol", 1)
    two_far = swap(two, "pol", 1)
    blocks = n_ma * n_pol
    left, share, weight = call(
        functools.partial(load_kernel, 3),
        (
            jax.ShapeDtypeStruct((blocks, modes, 2 * ell), beam.dtype),
            jax.ShapeDtypeStruct((n_pol, modes, 2 * ell), beam.dtype),
            weights,
        ),
        (),
        (pltpu.with_memory_space_constraint(response, pltpu.HBM), noise),
        0,
        in_specs=[HBM, VMEM],
        scratch_shapes=[pltpu.SemaphoreType.DMA((2 * blocks,))],
    )
    share = swap(share, "pol", 1)
    other_weight = swap(weight, "pol", 1)
    steps = ((0, 0), (0, 1), (1, 0), (1, 1), (2, 0), (2, 1))
    give, mine = (
        call(
            functools.partial(first_kernel, steps, other),
            visible(half),
            (m_table, chan_mask),
            (left, own, own_far, one, one_far, two, two_far),
            3,
        )
        for other in (1, 0)
    )
    got = swap(give, "pol", 1)
    mine, got = call(
        functools.partial(same_kernel, 3),
        (visible(half), visible(half)),
        (m_table,),
        (left, share, mine, got, same),
        1,
    )
    near, far, total = call(
        functools.partial(last_kernel, 3, n_freq),
        (visible(half), visible(half), row),
        (m_table, chan_mask),
        (left, share, weight, other_weight, mine, got, cross),
        1,
    )
    far = swap(far, "pol", 1)
    for name, step in (("pol", 1), ("freq", 1), ("ma", 3), ("ma", 1)):
        total = total + swap(total, name, step)
    scaled, own_power = call(
        functools.partial(finish_kernel, n_freq, n_ma * n_pol * modes * maps),
        (
            jax.ShapeDtypeStruct((parts, modes, maps), jnp.bfloat16),
            jax.ShapeDtypeStruct((1, 128), jnp.float32),
        ),
        (chan_mask,),
        (total, near, far),
        0,
        out_specs=(HBM, HBM),
        scratch_shapes=[
            pltpu.VMEM((n_pol, parts, modes, half), jnp.bfloat16),
            pltpu.VMEM((1, 128), jnp.float32),
            pltpu.SemaphoreType.DMA((4 * parts + 1,)),
        ],
    )
    return scaled[:, None, None], own_power[0, :1]


def on_device_plain(alm, beam, m_table, chan_mask, noise):
    arrived = lax.all_to_all(alm, "ma", split_axis=3, concat_axis=2, tiled=True)
    blocks = arrived.reshape(
        arrived.shape[0],
        arrived.shape[1],
        lax.axis_size("ma"),
        arrived.shape[2] // lax.axis_size("ma"),
        arrived.shape[4],
    )
    joined = lax.all_gather(blocks, "pol", axis=3, tiled=True)
    coeffs_all = joined.reshape(
        joined.shape[0], joined.shape[1], joined.shape[2] * joined.shape[3], joined.shape[4]
    )
    degree = lax.iota(jnp.int32, coeffs_all.shape[2])
    keep_mask = (degree >= m_table[0])[None, None, :, None]
    coeffs = jnp.where(keep_mask, coeffs_all, jnp.zeros((), coeffs_all.dtype))
    response = beam[0]
    real_part = jnp.einsum(
        "fkl,fls->fks", response[:, 0], coeffs[0], preferred_element_type=jnp.float32
    ) - jnp.einsum("fkl,fls->fks", response[:, 1], coeffs[1], preferred_element_type=jnp.float32)
    imag_part = jnp.einsum(
        "fkl,fls->fks", response[:, 0], coeffs[1], preferred_element_type=jnp.float32
    ) + jnp.einsum("fkl,fls->fks", response[:, 1], coeffs[0], preferred_element_type=jnp.float32)
    visibility = jnp.stack([real_part, imag_part])
    weighted = visibility * visibility / noise[None, :, :, None]
    partial_power = jnp.sum(weighted, axis=(0, 2, 3))
    modes_total = jnp.float32(
        lax.axis_size("ma") * noise.shape[1] * lax.axis_size("pol") * visibility.shape[3]
    )
    mask_float = chan_mask.astype(jnp.float32)
    channel_power = lax.psum(partial_power, ("ma", "pol")) / modes_total
    masked_sum, live_count = lax.psum(
        (jnp.sum(mask_float * channel_power), jnp.sum(mask_float)), "freq"
    )
    band_power = masked_sum / live_count
    factor = mask_float / jnp.sqrt(0.5 * channel_power + 0.5 * band_power + 1e-06)
    scaled = visibility * (lax.rsqrt(noise) * factor[:, None])[None, :, :, None]
    return (scaled[:, :, None].astype(jnp.bfloat16), channel_power)


def step(alm, beam, m_table, chan_mask, noise):
    sizes = [lax.axis_size(name) for name in ("ma", "freq", "pol")]
    if alm.shape[2] % 128 == 0 and sizes == [4, 2, 2]:
        return on_device(alm, beam, m_table, chan_mask, noise)
    return on_device_plain(alm, beam, m_table, chan_mask, noise)


def solution(mesh):
    return jax.shard_map(
        step,
        mesh=mesh,
        in_specs=(
            P(None, "freq", ("ma", "pol"), None, "sky"),
            P("ma", "freq", None, "pol", None),
            P("ma"),
            P("freq"),
            P("freq", "pol"),
        ),
        out_specs=(P(None, "freq", "ma", "pol", "sky"), P(("sky", "freq"))),
        check_vma=False,
    )
```

```python
import functools
import math

import jax
import jax.numpy as jnp
from jax import lax
from jax.experimental import pallas as pl
from jax.experimental.pallas import tpu as pltpu
from jax.sharding import PartitionSpec as P

VMEM = pl.BlockSpec(memory_space=pltpu.VMEM)
SMEM = pl.BlockSpec(memory_space=pltpu.SMEM)
HBM = pl.BlockSpec(memory_space=pltpu.HBM)


def column(row):
    return jnp.transpose(jnp.broadcast_to(row, (128, row.shape[1])))


def maps_of(pol, count):
    return pl.ds(pl.multiple_of(pol * count, count), count)


def split_kernel(pieces, alm_ref, *refs):
    *slab_refs, held_ref, modes_ref, sems = refs
    place, pol = lax.axis_index("ma"), lax.axis_index("pol")
    parts, ell = alm_ref.shape[:2]
    chunks = 2
    size = ell // chunks
    copies = {}
    for c in range(parts):
        for j in range(chunks):
            rows = pl.ds(j * size, size)
            copies[c, j] = pltpu.make_async_copy(
                alm_ref.at[c, rows], held_ref.at[c, rows], sems.at[c * chunks + j]
            )
            copies[c, j].start()
    for (c, j), copy in copies.items():
        copy.wait()
        rows = slice(j * size, (j + 1) * size)
        modes_ref[...] = pltpu.einshape("lms->mls", held_ref[c, rows])
        for ref, (step, other) in zip(slab_refs, pieces, strict=True):
            if other is None:
                ref[c, rows] = modes_ref[place ^ step]
            else:
                ref[c, rows] = modes_ref[place ^ step, :, maps_of(pol ^ other, ref.shape[2])]


def load_kernel(step, beam_ref, noise_ref, left_ref, share_ref, weight_ref, sems):
    blocks = left_ref.shape[0]
    ell = beam_ref.shape[2] // blocks
    copies = []
    for block in range(blocks):
        for c in range(2):
            copies.append(
                pltpu.make_async_copy(
                    beam_ref.at[c, :, pl.ds(block * ell, ell)],
                    left_ref.at[block, :, pl.ds(c * ell, ell)],
                    sems.at[2 * block + c],
                )
            )
            copies[-1].start()
    weight_ref[...] = column(lax.rsqrt(noise_ref[...]))
    for copy in copies:
        copy.wait()
    for half in range(share_ref.shape[0]):
        share_ref[half] = left_ref[(lax.axis_index("ma") ^ step) * lax.axis_size("pol") + half]


def operands(m_ref, block_refs, steps, maps):
    ell = block_refs[0].shape[1]
    blocks, right_real, right_imag = [], [], []
    for ref, (step, other) in zip(block_refs, steps, strict=True):
        owner = lax.axis_index("ma") ^ step
        half = lax.axis_index("pol") ^ other
        block = owner * lax.axis_size("pol") + half
        real, imag = ref[0, :, maps], ref[1, :, maps]
        degree = block * ell + lax.broadcasted_iota(jnp.int32, real.shape, 0)
        keep = degree >= m_ref[0]
        real = jnp.where(keep, real, jnp.zeros((), ref.dtype))
        imag = jnp.where(keep, imag, jnp.zeros((), ref.dtype))
        blocks.append(block)
        right_real += [real, -imag]
        right_imag += [imag, real]
    return blocks, jnp.concatenate(right_real, axis=0), jnp.concatenate(right_imag, axis=0)


dot = functools.partial(jnp.dot, preferred_element_type=jnp.float32)


def first_kernel(steps, other, m_ref, mask_ref, left_ref, *refs):
    del mask_ref
    *block_refs, vis_ref = refs
    maps = maps_of(lax.axis_index("pol") ^ other, vis_ref.shape[2])
    blocks, *rights = operands(m_ref, block_refs, steps, maps)
    left = jnp.concatenate([left_ref[block] for block in blocks], axis=1)
    for c, right in enumerate(rights):
        vis_ref[c] = dot(left, right)


def same_kernel(step, m_ref, left_ref, share_ref, mine_ref, got_ref, block_ref, near_ref, far_ref):
    (block,), *rights = operands(m_ref, [block_ref], [(step, 0)], slice(None))
    shared = share_ref[lax.axis_index("pol")]
    for c, right in enumerate(rights):
        near_ref[c] = mine_ref[c] + dot(left_ref[block], right)
        far_ref[c] = got_ref[c] + dot(shared, right)


def weigh(vis, weight):
    return jnp.concatenate(
        [vis[:, i : i + 128] * weight for i in range(0, vis.shape[1], 128)], axis=1
    )


def last_kernel(
    step,
    slots,
    m_ref,
    mask_ref,
    left_ref,
    share_ref,
    weight_ref,
    other_ref,
    mine_ref,
    got_ref,
    block_ref,
    near_ref,
    far_ref,
    power_ref,
):
    (block,), *rights = operands(m_ref, [block_ref], [(step, 1)], slice(None))
    sums = jnp.zeros(weight_ref.shape, jnp.float32)
    for left, before_ref, weights_ref, ref in (
        (share_ref[lax.axis_index("pol") ^ 1], got_ref, other_ref, far_ref),
        (left_ref[block], mine_ref, weight_ref, near_ref),
    ):
        weight = weights_ref[...]
        for c, right in enumerate(rights):
            vis = weigh(before_ref[c] + dot(left, right), weight)
            ref[c] = vis
            for i in range(0, vis.shape[1], 128):
                sums += vis[:, i : i + 128] * vis[:, i : i + 128]
    total = jnp.sum(sums)
    lane = lax.broadcasted_iota(jnp.int32, power_ref.shape, 1)
    leader = (lax.axis_index("ma") == 0) & (lax.axis_index("pol") == 0)
    live = jnp.where(leader, mask_ref[0], 0).astype(jnp.float32)
    channel = lax.axis_index("freq")
    power_ref[...] = jnp.where(lane == channel, total, 0.0) + jnp.where(
        lane == channel + slots, live, 0.0
    )


def finish_kernel(slots, modes, mask_ref, total_ref, near_ref, got_ref, scaled_ref, power_ref, held_ref, own_ref, sems):
    lane = lax.broadcasted_iota(jnp.int32, (1, 128), 1)
    totals = total_ref[0:1, :]
    powers = totals / modes
    masks = pltpu.roll(totals, 128 - slots, 1)

    def over(where, values):
        return jnp.sum(jnp.where(where, values, 0.0), axis=1, keepdims=True)

    band = over(lane < slots, powers * masks) / over(lane < slots, masks)
    own = over(lane == lax.axis_index("freq"), powers)
    mask = mask_ref[0].astype(jnp.float32)
    factor = mask / jnp.sqrt(0.5 * own + 0.5 * band + 1e-06)
    own_ref[...] = jnp.where(lane == 0, own, 0.0)
    copies = [pltpu.make_async_copy(own_ref, power_ref, sems.at[0])]
    copies[0].start()
    parts, rows, count = near_ref.shape
    pol = lax.axis_index("pol")
    chunk = rows // 2
    for c in range(parts):
        for j in range(0, rows, chunk):
            for half, (ref, owner) in enumerate(((near_ref, pol), (got_ref, pol ^ 1))):
                held_ref[half, c, j : j + chunk] = (ref[c, j : j + chunk] * factor).astype(
                    scaled_ref.dtype
                )
                copies.append(
                    pltpu.make_async_copy(
                        held_ref.at[half, c, pl.ds(j, chunk)],
                        scaled_ref.at[c, pl.ds(j, chunk), maps_of(owner, count)],
                        sems.at[len(copies)],
                    )
                )
                copies[-1].start()
    for copy in copies:
        copy.wait()


def straight(x, name, step):
    size = lax.axis_size(name)
    return lax.ppermute(x, name, [(i, i ^ step) for i in range(size)])


def swap(x, name, step):
    names, flip = ("pol", step) if name == "pol" else ((name, "pol"), 2 * step + 1)
    size = lax.axis_size(names)
    return lax.ppermute(x, names, [(i, i ^ flip) for i in range(size)])


def corner_swap(x):
    names = ("ma", "freq", "pol")
    sizes = [lax.axis_size(name) for name in names]
    flip = (sizes[1] + 1) * sizes[2] + 1
    return lax.ppermute(x, names, [(i, i ^ flip) for i in range(math.prod(sizes))])


def on_device(alm, beam, m_table, chan_mask, noise):
    n_ma, n_pol, n_freq = (lax.axis_size(name) for name in ("ma", "pol", "freq"))
    parts, _, ell, _, maps = alm.shape
    modes = beam.shape[3]
    response = beam[0, 0]
    params = pltpu.CompilerParams(vmem_limit_bytes=24 << 20)

    def visible(count):
        return jax.ShapeDtypeStruct((parts, modes, count), jnp.float32)

    def slab(count):
        return jax.ShapeDtypeStruct((parts, ell, count), alm.dtype)

    row = jax.ShapeDtypeStruct((8, 128), jnp.float32)
    weights = jax.ShapeDtypeStruct((modes, 128), jnp.float32)

    def call(kernel, out_shape, scalars, operands, blocks, **more):
        return pl.pallas_call(
            kernel,
            out_shape=out_shape,
            in_specs=more.pop("in_specs", [SMEM] * len(scalars) + [VMEM] * len(operands)),
            out_specs=more.pop("out_specs", jax.tree.map(lambda _: VMEM, out_shape)),
            compiler_params=more.pop("compiler_params", params),
            cost_estimate=pl.CostEstimate(
                flops=blocks * 2 * 4 * modes * maps * ell,
                bytes_accessed=(blocks + 4) * parts * ell * (maps + modes) * 2,
                transcendentals=0,
            ),
            **more,
        )(*scalars, *operands)

    half = maps // n_pol
    pieces = ((2, None), (1, None), (3, 0), (3, 1), (0, None))
    two, one, same, cross, own = call(
        functools.partial(split_kernel, pieces),
        [slab(maps if other is None else half) for _, other in pieces],
        (),
        (pltpu.with_memory_space_constraint(alm[:, 0], pltpu.HBM),),
        0,
        in_specs=[HBM],
        scratch_shapes=[
            pltpu.VMEM((parts, ell, n_ma, maps), alm.dtype),
            pltpu.VMEM((n_ma, ell // 2, maps), alm.dtype),
            pltpu.SemaphoreType.DMA((2 * parts,)),
        ],
    )
    two = straight(two, "ma", 2)
    one = straight(one, "ma", 1)
    same = straight(same, "ma", 3)
    cross = swap(cross, "ma", 3)
    own_far = swap(own, "pol", 1)
    one_far = swap(one, "pol", 1)
    two_far = swap(two, "pol", 1)
    blocks = n_ma * n_pol
    left, share, weight = call(
        functools.partial(load_kernel, 3),
        (
            jax.ShapeDtypeStruct((blocks, modes, 2 * ell), beam.dtype),
            jax.ShapeDtypeStruct((n_pol, modes, 2 * ell), beam.dtype),
            weights,
        ),
        (),
        (pltpu.with_memory_space_constraint(response, pltpu.HBM), noise),
        0,
        in_specs=[HBM, VMEM],
        scratch_shapes=[pltpu.SemaphoreType.DMA((2 * blocks,))],
    )
    share = swap(share, "pol", 1)
    other_weight = swap(weight, "pol", 1)
    steps = ((0, 0), (0, 1), (1, 0), (1, 1), (2, 0), (2, 1))
    give, mine = (
        call(
            functools.partial(first_kernel, steps, other),
            visible(half),
            (m_table, chan_mask),
            (left, own, own_far, one, one_far, two, two_far),
            3,
        )
        for other in (1, 0)
    )
    got = swap(give, "pol", 1)
    mine, got = call(
        functools.partial(same_kernel, 3),
        (visible(half), visible(half)),
        (m_table,),
        (left, share, mine, got, same),
        1,
    )
    near, far, total = call(
        functools.partial(last_kernel, 3, n_freq),
        (visible(half), visible(half), row),
        (m_table, chan_mask),
        (left, share, weight, other_weight, mine, got, cross),
        1,
    )
    far = swap(far, "pol", 1)
    for name, step in (("pol", 1), ("ma", 3)):
        total = total + swap(total, name, step)
    beside = swap(total, "ma", 1)
    across = swap(total, "freq", 1)
    corner = corner_swap(total)
    total = total + beside + across + corner
    scaled, own_power = call(
        functools.partial(finish_kernel, n_freq, n_ma * n_pol * modes * maps),
        (
            jax.ShapeDtypeStruct((parts, modes, maps), jnp.bfloat16),
            jax.ShapeDtypeStruct((1, 128), jnp.float32),
        ),
        (chan_mask,),
        (total, near, far),
        0,
        out_specs=(HBM, HBM),
        scratch_shapes=[
            pltpu.VMEM((n_pol, parts, modes, half), jnp.bfloat16),
            pltpu.VMEM((1, 128), jnp.float32),
            pltpu.SemaphoreType.DMA((4 * parts + 1,)),
        ],
    )
    return scaled[:, None, None], own_power[0, :1]


def on_device_plain(alm, beam, m_table, chan_mask, noise):
    arrived = lax.all_to_all(alm, "ma", split_axis=3, concat_axis=2, tiled=True)
    blocks = arrived.reshape(
        arrived.shape[0],
        arrived.shape[1],
        lax.axis_size("ma"),
        arrived.shape[2] // lax.axis_size("ma"),
        arrived.shape[4],
    )
    joined = lax.all_gather(blocks, "pol", axis=3, tiled=True)
    coeffs_all = joined.reshape(
        joined.shape[0], joined.shape[1], joined.shape[2] * joined.shape[3], joined.shape[4]
    )
    degree = lax.iota(jnp.int32, coeffs_all.shape[2])
    keep_mask = (degree >= m_table[0])[None, None, :, None]
    coeffs = jnp.where(keep_mask, coeffs_all, jnp.zeros((), coeffs_all.dtype))
    response = beam[0]
    real_part = jnp.einsum(
        "fkl,fls->fks", response[:, 0], coeffs[0], preferred_element_type=jnp.float32
    ) - jnp.einsum("fkl,fls->fks", response[:, 1], coeffs[1], preferred_element_type=jnp.float32)
    imag_part = jnp.einsum(
        "fkl,fls->fks", response[:, 0], coeffs[1], preferred_element_type=jnp.float32
    ) + jnp.einsum("fkl,fls->fks", response[:, 1], coeffs[0], preferred_element_type=jnp.float32)
    visibility = jnp.stack([real_part, imag_part])
    weighted = visibility * visibility / noise[None, :, :, None]
    partial_power = jnp.sum(weighted, axis=(0, 2, 3))
    modes_total = jnp.float32(
        lax.axis_size("ma") * noise.shape[1] * lax.axis_size("pol") * visibility.shape[3]
    )
    mask_float = chan_mask.astype(jnp.float32)
    channel_power = lax.psum(partial_power, ("ma", "pol")) / modes_total
    masked_sum, live_count = lax.psum(
        (jnp.sum(mask_float * channel_power), jnp.sum(mask_float)), "freq"
    )
    band_power = masked_sum / live_count
    factor = mask_float / jnp.sqrt(0.5 * channel_power + 0.5 * band_power + 1e-06)
    scaled = visibility * (lax.rsqrt(noise) * factor[:, None])[None, :, :, None]
    return (scaled[:, :, None].astype(jnp.bfloat16), channel_power)


def step(alm, beam, m_table, chan_mask, noise):
    sizes = [lax.axis_size(name) for name in ("ma", "freq", "pol")]
    if alm.shape[2] % 128 == 0 and sizes == [4, 2, 2]:
        return on_device(alm, beam, m_table, chan_mask, noise)
    return on_device_plain(alm, beam, m_table, chan_mask, noise)


def solution(mesh):
    return jax.shard_map(
        step,
        mesh=mesh,
        in_specs=(
            P(None, "freq", ("ma", "pol"), None, "sky"),
            P("ma", "freq", None, "pol", None),
            P("ma"),
            P("freq"),
            P("freq", "pol"),
        ),
        out_specs=(P(None, "freq", "ma", "pol", "sky"), P(("sky", "freq"))),
        check_vma=False,
    )
```

```python
import functools
import math

import jax
import jax.numpy as jnp
from jax import lax
from jax.experimental import pallas as pl
from jax.experimental.pallas import tpu as pltpu
from jax.sharding import PartitionSpec as P

VMEM = pl.BlockSpec(memory_space=pltpu.VMEM)
SMEM = pl.BlockSpec(memory_space=pltpu.SMEM)
HBM = pl.BlockSpec(memory_space=pltpu.HBM)


def column(row):
    return jnp.transpose(jnp.broadcast_to(row, (128, row.shape[1])))


def maps_of(pol, count):
    return pl.ds(pl.multiple_of(pol * count, count), count)


def split_kernel(pieces, alm_ref, *refs):
    *slab_refs, held_ref, modes_ref, sems = refs
    place, pol = lax.axis_index("ma"), lax.axis_index("pol")
    parts, ell = alm_ref.shape[:2]
    chunks = 2
    size = ell // chunks
    copies = {}
    for c in range(parts):
        for j in range(chunks):
            rows = pl.ds(j * size, size)
            copies[c, j] = pltpu.make_async_copy(
                alm_ref.at[c, rows], held_ref.at[c, rows], sems.at[c * chunks + j]
            )
            copies[c, j].start()
    for (c, j), copy in copies.items():
        copy.wait()
        rows = slice(j * size, (j + 1) * size)
        modes_ref[...] = pltpu.einshape("lms->mls", held_ref[c, rows])
        for ref, (step, other, start, half) in zip(slab_refs, pieces, strict=True):
            count = ref.shape[2]
            if other is None:
                ref[c, rows] = modes_ref[place ^ step]
            else:
                first = pl.multiple_of((pol ^ other) * half + start, 128)
                ref[c, rows] = modes_ref[place ^ step, :, pl.ds(first, count)]


def load_kernel(step, beam_ref, noise_ref, left_ref, share_ref, weight_ref, sems):
    blocks = left_ref.shape[0]
    ell = beam_ref.shape[2] // blocks
    copies = []
    for block in range(blocks):
        for c in range(2):
            copies.append(
                pltpu.make_async_copy(
                    beam_ref.at[c, :, pl.ds(block * ell, ell)],
                    left_ref.at[block, :, pl.ds(c * ell, ell)],
                    sems.at[2 * block + c],
                )
            )
            copies[-1].start()
    weight_ref[...] = column(lax.rsqrt(noise_ref[...]))
    for copy in copies:
        copy.wait()
    for half in range(share_ref.shape[0]):
        share_ref[half] = left_ref[(lax.axis_index("ma") ^ step) * lax.axis_size("pol") + half]


def operands(m_ref, block_refs, steps, maps):
    ell = block_refs[0].shape[1]
    blocks, right_real, right_imag = [], [], []
    for ref, (step, other) in zip(block_refs, steps, strict=True):
        owner = lax.axis_index("ma") ^ step
        half = lax.axis_index("pol") ^ other
        block = owner * lax.axis_size("pol") + half
        real, imag = ref[0, :, maps], ref[1, :, maps]
        degree = block * ell + lax.broadcasted_iota(jnp.int32, real.shape, 0)
        keep = degree >= m_ref[0]
        real = jnp.where(keep, real, jnp.zeros((), ref.dtype))
        imag = jnp.where(keep, imag, jnp.zeros((), ref.dtype))
        blocks.append(block)
        right_real += [real, -imag]
        right_imag += [imag, real]
    return blocks, jnp.concatenate(right_real, axis=0), jnp.concatenate(right_imag, axis=0)


dot = functools.partial(jnp.dot, preferred_element_type=jnp.float32)


def first_kernel(steps, other, m_ref, mask_ref, left_ref, *refs):
    del mask_ref
    *block_refs, vis_ref = refs
    maps = maps_of(lax.axis_index("pol") ^ other, vis_ref.shape[2])
    blocks, *rights = operands(m_ref, block_refs, steps, maps)
    left = jnp.concatenate([left_ref[block] for block in blocks], axis=1)
    for c, right in enumerate(rights):
        vis_ref[c] = dot(left, right)


def same_kernel(step, m_ref, left_ref, share_ref, mine_ref, got_ref, block_ref, *refs):
    (block,), *rights = operands(m_ref, [block_ref], [(step, 0)], slice(None))
    shared = share_ref[lax.axis_index("pol")]
    for before_ref, left, pieces in (
        (mine_ref, left_ref[block], refs[0::2]),
        (got_ref, shared, refs[1::2]),
    ):
        for c, right in enumerate(rights):
            vis = before_ref[c] + dot(left, right)
            start = 0
            for ref in pieces:
                end = start + ref.shape[2]
                ref[c] = vis[:, start:end]
                start = end


def weigh(vis, weight):
    return jnp.concatenate(
        [vis[:, i : i + 128] * weight for i in range(0, vis.shape[1], 128)], axis=1
    )


def whole(step, m_ref, left_ref, share_ref, weight_ref, other_ref, mine_ref, got_ref, block_ref, near_ref, far_ref):
    (block,), *rights = operands(m_ref, [block_ref], [(step, 1)], slice(None))
    right = jnp.concatenate(rights, axis=1)
    maps = near_ref.shape[2]
    sums = jnp.zeros(weight_ref.shape, jnp.float32)
    for left, before_ref, weights_ref, ref in (
        (share_ref[lax.axis_index("pol") ^ 1], got_ref, other_ref, far_ref),
        (left_ref[block], mine_ref, weight_ref, near_ref),
    ):
        weight = weights_ref[...]
        terms = dot(left, right)
        for c in range(len(rights)):
            vis = weigh(before_ref[c] + terms[:, c * maps : (c + 1) * maps], weight)
            ref[c] = vis
            for i in range(0, maps, 128):
                sums += vis[:, i : i + 128] * vis[:, i : i + 128]
    return jnp.sum(sums)


def piece_kernel(step, m_ref, *refs):
    *rest, power_ref = refs
    power_ref[...] = jnp.full(power_ref.shape, whole(step, m_ref, *rest))


def last_kernel(step, slots, m_ref, mask_ref, early_ref, *refs):
    *rest, power_ref = refs
    total = early_ref[...] + whole(step, m_ref, *rest)
    lane = lax.broadcasted_iota(jnp.int32, power_ref.shape, 1)
    leader = (lax.axis_index("ma") == 0) & (lax.axis_index("pol") == 0)
    live = jnp.where(leader, mask_ref[0], 0).astype(jnp.float32)
    channel = lax.axis_index("freq")
    power_ref[...] = jnp.where(lane == channel, total, 0.0) + jnp.where(
        lane == channel + slots, live, 0.0
    )


def finish_kernel(slots, modes, mask_ref, total_ref, near_a, got_a, near_b, got_b, scaled_ref, power_ref, held_ref, own_ref, sems):
    lane = lax.broadcasted_iota(jnp.int32, (1, 128), 1)
    totals = total_ref[0:1, :]
    powers = totals / modes
    masks = pltpu.roll(totals, 128 - slots, 1)

    def over(where, values):
        return jnp.sum(jnp.where(where, values, 0.0), axis=1, keepdims=True)

    band = over(lane < slots, powers * masks) / over(lane < slots, masks)
    own = over(lane == lax.axis_index("freq"), powers)
    mask = mask_ref[0].astype(jnp.float32)
    factor = mask / jnp.sqrt(0.5 * own + 0.5 * band + 1e-06)
    own_ref[...] = jnp.where(lane == 0, own, 0.0)
    copies = [pltpu.make_async_copy(own_ref, power_ref, sems.at[0])]
    copies[0].start()
    _, parts, rows, count = held_ref.shape
    pol = lax.axis_index("pol")
    chunk = rows // 2
    for c in range(parts):
        for j in range(0, rows, chunk):
            for half, (pieces, owner) in enumerate(
                (((near_a, near_b), pol), ((got_a, got_b), pol ^ 1))
            ):
                start = 0
                for ref in pieces:
                    end = start + ref.shape[2]
                    held_ref[half, c, j : j + chunk, start:end] = (
                        ref[c, j : j + chunk] * factor
                    ).astype(scaled_ref.dtype)
                    start = end
                copies.append(
                    pltpu.make_async_copy(
                        held_ref.at[half, c, pl.ds(j, chunk)],
                        scaled_ref.at[c, pl.ds(j, chunk), maps_of(owner, count)],
                        sems.at[len(copies)],
                    )
                )
                copies[-1].start()
    for copy in copies:
        copy.wait()


def straight(x, name, step):
    size = lax.axis_size(name)
    return lax.ppermute(x, name, [(i, i ^ step) for i in range(size)])


def swap(x, name, step):
    names, flip = ("pol", step) if name == "pol" else ((name, "pol"), 2 * step + 1)
    size = lax.axis_size(names)
    return lax.ppermute(x, names, [(i, i ^ flip) for i in range(size)])


def corner_swap(x):
    names = ("ma", "freq", "pol")
    sizes = [lax.axis_size(name) for name in names]
    flip = (sizes[1] + 1) * sizes[2] + 1
    return lax.ppermute(x, names, [(i, i ^ flip) for i in range(math.prod(sizes))])


def on_device(alm, beam, m_table, chan_mask, noise):
    n_ma, n_pol, n_freq = (lax.axis_size(name) for name in ("ma", "pol", "freq"))
    parts, _, ell, _, maps = alm.shape
    modes = beam.shape[3]
    response = beam[0, 0]
    params = pltpu.CompilerParams(vmem_limit_bytes=24 << 20)

    def visible(count):
        return jax.ShapeDtypeStruct((parts, modes, count), jnp.float32)

    def slab(count):
        return jax.ShapeDtypeStruct((parts, ell, count), alm.dtype)

    row = jax.ShapeDtypeStruct((1, 128), jnp.float32)
    weights = jax.ShapeDtypeStruct((modes, 128), jnp.float32)

    def call(kernel, out_shape, scalars, operands, blocks, **more):
        return pl.pallas_call(
            kernel,
            out_shape=out_shape,
            in_specs=more.pop("in_specs", [SMEM] * len(scalars) + [VMEM] * len(operands)),
            out_specs=more.pop("out_specs", jax.tree.map(lambda _: VMEM, out_shape)),
            compiler_params=more.pop("compiler_params", params),
            cost_estimate=pl.CostEstimate(
                flops=blocks * 2 * 4 * modes * maps * ell,
                bytes_accessed=(blocks + 4) * parts * ell * (maps + modes) * 2,
                transcendentals=0,
            ),
            **more,
        )(*scalars, *operands)

    half = maps // n_pol
    early = half // 2 // 128 * 128 or half
    late = half - early
    pieces = (
        (2, None, 0, maps),
        (1, None, 0, maps),
        (3, 0, 0, half),
        (3, 1, 0, half),
        (3, 1, early, half),
        (0, None, 0, maps),
    )
    two, one, same, cross_a, cross_b, own = call(
        functools.partial(split_kernel, pieces),
        [slab(count) for count in (maps, maps, half, early, late, maps)],
        (),
        (pltpu.with_memory_space_constraint(alm[:, 0], pltpu.HBM),),
        0,
        in_specs=[HBM],
        scratch_shapes=[
            pltpu.VMEM((parts, ell, n_ma, maps), alm.dtype),
            pltpu.VMEM((n_ma, ell // 2, maps), alm.dtype),
            pltpu.SemaphoreType.DMA((2 * parts,)),
        ],
    )
    two = straight(two, "ma", 2)
    one = straight(one, "ma", 1)
    same = straight(same, "ma", 3)
    cross_a = swap(cross_a, "ma", 3)
    cross_b = swap(cross_b, "ma", 3)
    own_far = swap(own, "pol", 1)
    one_far = swap(one, "pol", 1)
    two_far = swap(two, "pol", 1)
    blocks = n_ma * n_pol
    left, share, weight = call(
        functools.partial(load_kernel, 3),
        (
            jax.ShapeDtypeStruct((blocks, modes, 2 * ell), beam.dtype),
            jax.ShapeDtypeStruct((n_pol, modes, 2 * ell), beam.dtype),
            weights,
        ),
        (),
        (pltpu.with_memory_space_constraint(response, pltpu.HBM), noise),
        0,
        in_specs=[HBM, VMEM],
        scratch_shapes=[pltpu.SemaphoreType.DMA((2 * blocks,))],
    )
    share = swap(share, "pol", 1)
    other_weight = swap(weight, "pol", 1)
    steps = ((0, 0), (0, 1), (1, 0), (1, 1), (2, 0), (2, 1))
    give, mine = (
        call(
            functools.partial(first_kernel, steps, other),
            visible(half),
            (m_table, chan_mask),
            (left, own, own_far, one, one_far, two, two_far),
            3,
        )
        for other in (1, 0)
    )
    got = swap(give, "pol", 1)
    mine_a, got_a, mine_b, got_b = call(
        functools.partial(same_kernel, 3),
        [visible(early), visible(early), visible(late), visible(late)],
        (m_table,),
        (left, share, mine, got, same),
        1,
    )
    near_a, far_a, power = call(
        functools.partial(piece_kernel, 3),
        (visible(early), visible(early), row),
        (m_table,),
        (left, share, weight, other_weight, mine_a, got_a, cross_a),
        1,
    )
    far_a = swap(far_a, "pol", 1)
    near_b, far_b, total = call(
        functools.partial(last_kernel, 3, n_freq),
        (visible(late), visible(late), row),
        (m_table, chan_mask),
        (power, left, share, weight, other_weight, mine_b, got_b, cross_b),
        1,
    )
    far_b = swap(far_b, "pol", 1)
    for name, step in (("pol", 1), ("ma", 3)):
        total = total + swap(total, name, step)
    beside = swap(total, "ma", 1)
    across = swap(total, "freq", 1)
    corner = corner_swap(total)
    total = total + beside + across + corner
    scaled, own_power = call(
        functools.partial(finish_kernel, n_freq, n_ma * n_pol * modes * maps),
        (
            jax.ShapeDtypeStruct((parts, modes, maps), jnp.bfloat16),
            jax.ShapeDtypeStruct((1, 128), jnp.float32),
        ),
        (chan_mask,),
        (total, near_a, far_a, near_b, far_b),
        0,
        out_specs=(HBM, HBM),
        scratch_shapes=[
            pltpu.VMEM((n_pol, parts, modes, half), jnp.bfloat16),
            pltpu.VMEM((1, 128), jnp.float32),
            pltpu.SemaphoreType.DMA((4 * parts + 1,)),
        ],
    )
    return scaled[:, None, None], own_power[0, :1]


def on_device_plain(alm, beam, m_table, chan_mask, noise):
    arrived = lax.all_to_all(alm, "ma", split_axis=3, concat_axis=2, tiled=True)
    blocks = arrived.reshape(
        arrived.shape[0],
        arrived.shape[1],
        lax.axis_size("ma"),
        arrived.shape[2] // lax.axis_size("ma"),
        arrived.shape[4],
    )
    joined = lax.all_gather(blocks, "pol", axis=3, tiled=True)
    coeffs_all = joined.reshape(
        joined.shape[0], joined.shape[1], joined.shape[2] * joined.shape[3], joined.shape[4]
    )
    degree = lax.iota(jnp.int32, coeffs_all.shape[2])
    keep_mask = (degree >= m_table[0])[None, None, :, None]
    coeffs = jnp.where(keep_mask, coeffs_all, jnp.zeros((), coeffs_all.dtype))
    response = beam[0]
    real_part = jnp.einsum(
        "fkl,fls->fks", response[:, 0], coeffs[0], preferred_element_type=jnp.float32
    ) - jnp.einsum("fkl,fls->fks", response[:, 1], coeffs[1], preferred_element_type=jnp.float32)
    imag_part = jnp.einsum(
        "fkl,fls->fks", response[:, 0], coeffs[1], preferred_element_type=jnp.float32
    ) + jnp.einsum("fkl,fls->fks", response[:, 1], coeffs[0], preferred_element_type=jnp.float32)
    visibility = jnp.stack([real_part, imag_part])
    weighted = visibility * visibility / noise[None, :, :, None]
    partial_power = jnp.sum(weighted, axis=(0, 2, 3))
    modes_total = jnp.float32(
        lax.axis_size("ma") * noise.shape[1] * lax.axis_size("pol") * visibility.shape[3]
    )
    mask_float = chan_mask.astype(jnp.float32)
    channel_power = lax.psum(partial_power, ("ma", "pol")) / modes_total
    masked_sum, live_count = lax.psum(
        (jnp.sum(mask_float * channel_power), jnp.sum(mask_float)), "freq"
    )
    band_power = masked_sum / live_count
    factor = mask_float / jnp.sqrt(0.5 * channel_power + 0.5 * band_power + 1e-06)
    scaled = visibility * (lax.rsqrt(noise) * factor[:, None])[None, :, :, None]
    return (scaled[:, :, None].astype(jnp.bfloat16), channel_power)


def step(alm, beam, m_table, chan_mask, noise):
    sizes = [lax.axis_size(name) for name in ("ma", "freq", "pol")]
    if alm.shape[2] % 128 == 0 and sizes == [4, 2, 2]:
        return on_device(alm, beam, m_table, chan_mask, noise)
    return on_device_plain(alm, beam, m_table, chan_mask, noise)


def solution(mesh):
    return jax.shard_map(
        step,
        mesh=mesh,
        in_specs=(
            P(None, "freq", ("ma", "pol"), None, "sky"),
            P("ma", "freq", None, "pol", None),
            P("ma"),
            P("freq"),
            P("freq", "pol"),
        ),
        out_specs=(P(None, "freq", "ma", "pol", "sky"), P(("sky", "freq"))),
        check_vma=False,
    )
```

```python
import functools
import math

import jax
import jax.numpy as jnp
from jax import lax
from jax.experimental import pallas as pl
from jax.experimental.pallas import tpu as pltpu
from jax.sharding import PartitionSpec as P

VMEM = pl.BlockSpec(memory_space=pltpu.VMEM)
SMEM = pl.BlockSpec(memory_space=pltpu.SMEM)
HBM = pl.BlockSpec(memory_space=pltpu.HBM)


def column(row):
    return jnp.transpose(jnp.broadcast_to(row, (128, row.shape[1])))


def maps_of(pol, count):
    return pl.ds(pl.multiple_of(pol * count, count), count)


def split_kernel(pieces, alm_ref, *refs):
    *slab_refs, held_ref, modes_ref, sems = refs
    place, pol = lax.axis_index("ma"), lax.axis_index("pol")
    parts, ell = alm_ref.shape[:2]
    chunks = 2
    size = ell // chunks
    copies = {}
    for c in range(parts):
        for j in range(chunks):
            rows = pl.ds(j * size, size)
            copies[c, j] = pltpu.make_async_copy(
                alm_ref.at[c, rows], held_ref.at[c, rows], sems.at[c * chunks + j]
            )
            copies[c, j].start()
    for (c, j), copy in copies.items():
        copy.wait()
        rows = slice(j * size, (j + 1) * size)
        modes_ref[...] = pltpu.einshape("lms->mls", held_ref[c, rows])
        for ref, (step, other, start, half) in zip(slab_refs, pieces, strict=True):
            count = ref.shape[2]
            if other is None:
                ref[c, rows] = modes_ref[place ^ step]
            else:
                first = pl.multiple_of((pol ^ other) * half + start, 128)
                ref[c, rows] = modes_ref[place ^ step, :, pl.ds(first, count)]


def load_kernel(step, beam_ref, noise_ref, left_ref, share_ref, weight_ref, sems):
    blocks = left_ref.shape[0]
    ell = beam_ref.shape[2] // blocks
    copies = []
    for block in range(blocks):
        for c in range(2):
            copies.append(
                pltpu.make_async_copy(
                    beam_ref.at[c, :, pl.ds(block * ell, ell)],
                    left_ref.at[block, :, pl.ds(c * ell, ell)],
                    sems.at[2 * block + c],
                )
            )
            copies[-1].start()
    weight_ref[...] = column(lax.rsqrt(noise_ref[...]))
    for copy in copies:
        copy.wait()
    for half in range(share_ref.shape[0]):
        share_ref[half] = left_ref[(lax.axis_index("ma") ^ step) * lax.axis_size("pol") + half]


def operands(m_ref, block_refs, steps, maps):
    ell = block_refs[0].shape[1]
    blocks, right_real, right_imag = [], [], []
    for ref, (step, other) in zip(block_refs, steps, strict=True):
        owner = lax.axis_index("ma") ^ step
        half = lax.axis_index("pol") ^ other
        block = owner * lax.axis_size("pol") + half
        real, imag = ref[0, :, maps], ref[1, :, maps]
        degree = block * ell + lax.broadcasted_iota(jnp.int32, real.shape, 0)
        keep = degree >= m_ref[0]
        real = jnp.where(keep, real, jnp.zeros((), ref.dtype))
        imag = jnp.where(keep, imag, jnp.zeros((), ref.dtype))
        blocks.append(block)
        right_real += [real, -imag]
        right_imag += [imag, real]
    return blocks, jnp.concatenate(right_real, axis=0), jnp.concatenate(right_imag, axis=0)


dot = functools.partial(jnp.dot, preferred_element_type=jnp.float32)


def first_kernel(steps, other, m_ref, mask_ref, left_ref, *refs):
    del mask_ref
    *block_refs, vis_ref = refs
    maps = maps_of(lax.axis_index("pol") ^ other, vis_ref.shape[2])
    blocks, *rights = operands(m_ref, block_refs, steps, maps)
    left = jnp.concatenate([left_ref[block] for block in blocks], axis=1)
    for c, right in enumerate(rights):
        vis_ref[c] = dot(left, right)


def same_kernel(step, m_ref, left_ref, share_ref, mine_ref, got_ref, block_ref, *refs):
    (block,), *rights = operands(m_ref, [block_ref], [(step, 0)], slice(None))
    shared = share_ref[lax.axis_index("pol")]
    for before_ref, left, pieces in (
        (mine_ref, left_ref[block], refs[0::2]),
        (got_ref, shared, refs[1::2]),
    ):
        for c, right in enumerate(rights):
            vis = before_ref[c] + dot(left, right)
            start = 0
            for ref in pieces:
                end = start + ref.shape[2]
                ref[c] = vis[:, start:end]
                start = end


def weigh(vis, weight):
    return jnp.concatenate(
        [vis[:, i : i + 128] * weight for i in range(0, vis.shape[1], 128)], axis=1
    )


def whole(step, m_ref, left_ref, share_ref, weight_ref, other_ref, mine_ref, got_ref, block_ref, near_ref, far_ref):
    (block,), *rights = operands(m_ref, [block_ref], [(step, 1)], slice(None))
    right = jnp.concatenate(rights, axis=1)
    maps = near_ref.shape[2]
    sums = jnp.zeros(weight_ref.shape, jnp.float32)
    for left, before_ref, weights_ref, ref in (
        (share_ref[lax.axis_index("pol") ^ 1], got_ref, other_ref, far_ref),
        (left_ref[block], mine_ref, weight_ref, near_ref),
    ):
        weight = weights_ref[...]
        terms = dot(left, right)
        for c in range(len(rights)):
            vis = weigh(before_ref[c] + terms[:, c * maps : (c + 1) * maps], weight)
            ref[c] = vis
            for i in range(0, maps, 128):
                sums += vis[:, i : i + 128] * vis[:, i : i + 128]
    return jnp.sum(sums, axis=0, keepdims=True)


def piece_kernel(step, m_ref, *refs):
    *rest, power_ref = refs
    power_ref[...] = whole(step, m_ref, *rest)


def last_kernel(step, slots, m_ref, mask_ref, early_ref, *refs):
    *rest, power_ref = refs
    total = early_ref[...] + whole(step, m_ref, *rest)
    place = lax.broadcasted_iota(jnp.int32, power_ref.shape, 0)
    lane = lax.broadcasted_iota(jnp.int32, power_ref.shape, 1)
    leader = (lax.axis_index("ma") == 0) & (lax.axis_index("pol") == 0)
    live = jnp.where(leader, mask_ref[0], 0).astype(jnp.float32)
    channel = lax.axis_index("freq")
    power_ref[...] = jnp.where(place == channel, total, 0.0) + jnp.where(
        (place == channel + slots) & (lane == 0), live, 0.0
    )


def finish_kernel(slots, modes, mask_ref, total_ref, near_a, got_a, near_b, got_b, scaled_ref, power_ref, held_ref, own_ref, sems):
    lane = lax.broadcasted_iota(jnp.int32, (1, 128), 1)
    powers = jnp.sum(total_ref[:slots], axis=1, keepdims=True) / modes
    masks = jnp.sum(total_ref[slots:], axis=1, keepdims=True)
    place = lax.broadcasted_iota(jnp.int32, powers.shape, 0)
    band = jnp.sum(powers * masks, axis=0, keepdims=True) / jnp.sum(masks, axis=0, keepdims=True)
    own = jnp.sum(
        jnp.where(place == lax.axis_index("freq"), powers, 0.0), axis=0, keepdims=True
    )
    mask = mask_ref[0].astype(jnp.float32)
    factor = mask * lax.rsqrt(0.5 * own + 0.5 * band + 1e-06)
    own_ref[...] = jnp.where(lane == 0, own, 0.0)
    copies = [pltpu.make_async_copy(own_ref, power_ref, sems.at[0])]
    copies[0].start()
    _, parts, rows, count = held_ref.shape
    pol = lax.axis_index("pol")
    chunk = rows // 2
    for c in range(parts):
        for j in range(0, rows, chunk):
            for half, (pieces, owner) in enumerate(
                (((near_a, near_b), pol), ((got_a, got_b), pol ^ 1))
            ):
                start = 0
                for ref in pieces:
                    end = start + ref.shape[2]
                    held_ref[half, c, j : j + chunk, start:end] = (
                        ref[c, j : j + chunk] * factor
                    ).astype(scaled_ref.dtype)
                    start = end
                copies.append(
                    pltpu.make_async_copy(
                        held_ref.at[half, c, pl.ds(j, chunk)],
                        scaled_ref.at[c, pl.ds(j, chunk), maps_of(owner, count)],
                        sems.at[len(copies)],
                    )
                )
                copies[-1].start()
    for copy in copies:
        copy.wait()


def straight(x, name, step):
    size = lax.axis_size(name)
    return lax.ppermute(x, name, [(i, i ^ step) for i in range(size)])


def swap(x, name, step):
    names, flip = ("pol", step) if name == "pol" else ((name, "pol"), 2 * step + 1)
    size = lax.axis_size(names)
    return lax.ppermute(x, names, [(i, i ^ flip) for i in range(size)])


def corner_swap(x):
    names = ("ma", "freq", "pol")
    sizes = [lax.axis_size(name) for name in names]
    flip = (sizes[1] + 1) * sizes[2] + 1
    return lax.ppermute(x, names, [(i, i ^ flip) for i in range(math.prod(sizes))])


def on_device(alm, beam, m_table, chan_mask, noise):
    n_ma, n_pol, n_freq = (lax.axis_size(name) for name in ("ma", "pol", "freq"))
    parts, _, ell, _, maps = alm.shape
    modes = beam.shape[3]
    response = beam[0, 0]
    params = pltpu.CompilerParams(vmem_limit_bytes=24 << 20)

    def visible(count):
        return jax.ShapeDtypeStruct((parts, modes, count), jnp.float32)

    def slab(count):
        return jax.ShapeDtypeStruct((parts, ell, count), alm.dtype)

    row = jax.ShapeDtypeStruct((1, 128), jnp.float32)
    weights = jax.ShapeDtypeStruct((modes, 128), jnp.float32)

    def call(kernel, out_shape, scalars, operands, blocks, **more):
        return pl.pallas_call(
            kernel,
            out_shape=out_shape,
            in_specs=more.pop("in_specs", [SMEM] * len(scalars) + [VMEM] * len(operands)),
            out_specs=more.pop("out_specs", jax.tree.map(lambda _: VMEM, out_shape)),
            compiler_params=more.pop("compiler_params", params),
            cost_estimate=pl.CostEstimate(
                flops=blocks * 2 * 4 * modes * maps * ell,
                bytes_accessed=(blocks + 4) * parts * ell * (maps + modes) * 2,
                transcendentals=0,
            ),
            **more,
        )(*scalars, *operands)

    half = maps // n_pol
    early = half // 2 // 128 * 128 or half
    late = half - early
    pieces = (
        (2, None, 0, maps),
        (1, None, 0, maps),
        (3, 0, 0, half),
        (3, 1, 0, half),
        (3, 1, early, half),
        (0, None, 0, maps),
    )
    two, one, same, cross_a, cross_b, own = call(
        functools.partial(split_kernel, pieces),
        [slab(count) for count in (maps, maps, half, early, late, maps)],
        (),
        (pltpu.with_memory_space_constraint(alm[:, 0], pltpu.HBM),),
        0,
        in_specs=[HBM],
        scratch_shapes=[
            pltpu.VMEM((parts, ell, n_ma, maps), alm.dtype),
            pltpu.VMEM((n_ma, ell // 2, maps), alm.dtype),
            pltpu.SemaphoreType.DMA((2 * parts,)),
        ],
    )
    two = straight(two, "ma", 2)
    one = straight(one, "ma", 1)
    same = straight(same, "ma", 3)
    cross_a = swap(cross_a, "ma", 3)
    cross_b = swap(cross_b, "ma", 3)
    own_far = swap(own, "pol", 1)
    one_far = swap(one, "pol", 1)
    two_far = swap(two, "pol", 1)
    blocks = n_ma * n_pol
    left, share, weight = call(
        functools.partial(load_kernel, 3),
        (
            jax.ShapeDtypeStruct((blocks, modes, 2 * ell), beam.dtype),
            jax.ShapeDtypeStruct((n_pol, modes, 2 * ell), beam.dtype),
            weights,
        ),
        (),
        (pltpu.with_memory_space_constraint(response, pltpu.HBM), noise),
        0,
        in_specs=[HBM, VMEM],
        scratch_shapes=[pltpu.SemaphoreType.DMA((2 * blocks,))],
    )
    share = swap(share, "pol", 1)
    other_weight = swap(weight, "pol", 1)
    steps = ((0, 0), (0, 1), (1, 0), (1, 1), (2, 0), (2, 1))
    give, mine = (
        call(
            functools.partial(first_kernel, steps, other),
            visible(half),
            (m_table, chan_mask),
            (left, own, own_far, one, one_far, two, two_far),
            3,
        )
        for other in (1, 0)
    )
    got = swap(give, "pol", 1)
    mine_a, got_a, mine_b, got_b = call(
        functools.partial(same_kernel, 3),
        [visible(early), visible(early), visible(late), visible(late)],
        (m_table,),
        (left, share, mine, got, same),
        1,
    )
    near_a, far_a, power = call(
        functools.partial(piece_kernel, 3),
        (visible(early), visible(early), row),
        (m_table,),
        (left, share, weight, other_weight, mine_a, got_a, cross_a),
        1,
    )
    far_a = swap(far_a, "pol", 1)
    near_b, far_b, total = call(
        functools.partial(last_kernel, 3, n_freq),
        (visible(late), visible(late), jax.ShapeDtypeStruct((2 * n_freq, 128), jnp.float32)),
        (m_table, chan_mask),
        (power, left, share, weight, other_weight, mine_b, got_b, cross_b),
        1,
    )
    far_b = swap(far_b, "pol", 1)
    for name, step in (("pol", 1), ("ma", 3)):
        total = total + swap(total, name, step)
    beside = swap(total, "ma", 1)
    across = swap(total, "freq", 1)
    corner = corner_swap(total)
    total = total + beside + across + corner
    scaled, own_power = call(
        functools.partial(finish_kernel, n_freq, n_ma * n_pol * modes * maps),
        (
            jax.ShapeDtypeStruct((parts, modes, maps), jnp.bfloat16),
            jax.ShapeDtypeStruct((1, 128), jnp.float32),
        ),
        (chan_mask,),
        (total, near_a, far_a, near_b, far_b),
        0,
        out_specs=(HBM, HBM),
        scratch_shapes=[
            pltpu.VMEM((n_pol, parts, modes, half), jnp.bfloat16),
            pltpu.VMEM((1, 128), jnp.float32),
            pltpu.SemaphoreType.DMA((4 * parts + 1,)),
        ],
    )
    return scaled[:, None, None], own_power[0, :1]


def on_device_plain(alm, beam, m_table, chan_mask, noise):
    arrived = lax.all_to_all(alm, "ma", split_axis=3, concat_axis=2, tiled=True)
    blocks = arrived.reshape(
        arrived.shape[0],
        arrived.shape[1],
        lax.axis_size("ma"),
        arrived.shape[2] // lax.axis_size("ma"),
        arrived.shape[4],
    )
    joined = lax.all_gather(blocks, "pol", axis=3, tiled=True)
    coeffs_all = joined.reshape(
        joined.shape[0], joined.shape[1], joined.shape[2] * joined.shape[3], joined.shape[4]
    )
    degree = lax.iota(jnp.int32, coeffs_all.shape[2])
    keep_mask = (degree >= m_table[0])[None, None, :, None]
    coeffs = jnp.where(keep_mask, coeffs_all, jnp.zeros((), coeffs_all.dtype))
    response = beam[0]
    real_part = jnp.einsum(
        "fkl,fls->fks", response[:, 0], coeffs[0], preferred_element_type=jnp.float32
    ) - jnp.einsum("fkl,fls->fks", response[:, 1], coeffs[1], preferred_element_type=jnp.float32)
    imag_part = jnp.einsum(
        "fkl,fls->fks", response[:, 0], coeffs[1], preferred_element_type=jnp.float32
    ) + jnp.einsum("fkl,fls->fks", response[:, 1], coeffs[0], preferred_element_type=jnp.float32)
    visibility = jnp.stack([real_part, imag_part])
    weighted = visibility * visibility / noise[None, :, :, None]
    partial_power = jnp.sum(weighted, axis=(0, 2, 3))
    modes_total = jnp.float32(
        lax.axis_size("ma") * noise.shape[1] * lax.axis_size("pol") * visibility.shape[3]
    )
    mask_float = chan_mask.astype(jnp.float32)
    channel_power = lax.psum(partial_power, ("ma", "pol")) / modes_total
    masked_sum, live_count = lax.psum(
        (jnp.sum(mask_float * channel_power), jnp.sum(mask_float)), "freq"
    )
    band_power = masked_sum / live_count
    factor = mask_float / jnp.sqrt(0.5 * channel_power + 0.5 * band_power + 1e-06)
    scaled = visibility * (lax.rsqrt(noise) * factor[:, None])[None, :, :, None]
    return (scaled[:, :, None].astype(jnp.bfloat16), channel_power)


def step(alm, beam, m_table, chan_mask, noise):
    sizes = [lax.axis_size(name) for name in ("ma", "freq", "pol")]
    if alm.shape[2] % 128 == 0 and sizes == [4, 2, 2]:
        return on_device(alm, beam, m_table, chan_mask, noise)
    return on_device_plain(alm, beam, m_table, chan_mask, noise)


def solution(mesh):
    return jax.shard_map(
        step,
        mesh=mesh,
        in_specs=(
            P(None, "freq", ("ma", "pol"), None, "sky"),
            P("ma", "freq", None, "pol", None),
            P("ma"),
            P("freq"),
            P("freq", "pol"),
        ),
        out_specs=(P(None, "freq", "ma", "pol", "sky"), P(("sky", "freq"))),
        check_vma=False,
    )
```
